128 devices in a mesh: slave: 16 (over y, z), master: 8 (over x, core).
Axes of the slice: x: 4, y: 4, z: 4, core: 2. Of those that a mesh axis runs over, the one named last changes fastest.
Arguments:
- slave_basis: bfloat16 [256, 128, 128], P('slave'), may hold values from -1.5 to 1.5
- master_basis: bfloat16 [512, 128, 128], P(('slave', 'master')), may hold values from -1.5 to 1.5
- slave_gap: float32 [256, 128], P('slave'), may hold values from -6 to 6
- master_disp: float32 [512, 128], P(('slave', 'master')), may hold values from -6 to 6
- pressure: float32 [256, 128], P('slave'), may hold values from -6 to 6
- active: int32 [256, 128], P('slave'), may hold values 0 or 1
- need_owner: int32 [16384, 1], P(('slave', 'master')), may hold values from 0 to 127; in each aligned block of 128 rows (0 to 127, 128 to 255, ...) at most 2 rows name the same one
- need_slot: int32 [16384], P(('slave', 'master')), may hold values from 0 to 3
- pair_need: int32 [65536], P(('slave', 'master')), may hold values from 0 to 127
- pair_slave: int32 [65536], P(('slave', 'master')), may hold values from 0 to 15
- pair_segs: int32 [65536], P(('slave', 'master')), may hold values from 1 to 8
- pair_weight: float32 [65536, 128], P(('slave', 'master')), may hold values from 0.05 to 0.5
Outputs:
- pressure_out: float32 [256, 128], P('slave')
- disp_out: float32 [512, 128], P(('slave', 'master'))
- tile_out: bfloat16 [65536, 128, 128], P(('slave', 'master'))
The draws below stay inside these ranges and needn't reach their ends.
Inputs may be any that keep to these rules, and one draw needn't show every extreme that they name: `need_owner`: among the 128 requests of one device no owner is named more than 2 times, a bound that some block reaches.
All inputs are finite; a program needn't handle non-finite values. No bound on the sum of `active` on one device may be relied on, other than what follows from the above.
Results may differ from the reference program's by a relative error of at most 0.0049.
Values may be sent and summed in bfloat16 or wider, within the bound.
A program may use at most 128 MiB of HBM per device.

```python
import math
import jax
import jax.numpy as jnp
import numpy as np
from jax import lax

NODES = 128
SEGS = 8
GAUSS = 16
QPTS = 128
ITERS = 2
SB_DEV = 16
MB_DEV = 4
NEED_DEV = 128
PAIR_DEV = 512
CAP = 2
SBLOCKS = 256
MBLOCKS = 512
NEEDS = 16384
PAIRS = 65536
N_SLAVE = 16
N_MASTER = 8


def plant(values, own_key, smallest, high):
    longest = values.shape.index(max(values.shape))
    spots = []
    for shift in (0, 1):
        where = [jax.random.randint(jax.random.fold_in(own_key, axis), (), 0, length) for axis, length in enumerate(values.shape)]
        where[longest] = (where[longest] + shift) % values.shape[longest]
        spots.append(tuple(where))
    return values.at[spots[0]].set(smallest).at[spots[1]].set(high)


def steps_of(stream_key, extent, pieces, least, high):
    factor_of = 1.0
    for axis_at, blocks in pieces:
        steps = jax.random.uniform(jax.random.fold_in(jax.random.fold_in(stream_key, 6), axis_at), (blocks,), jnp.float32, least / len(pieces), high / len(pieces))
        factor_of = factor_of * jnp.repeat(jnp.exp(steps), extent[axis_at] // blocks).reshape((-1,) + (1,) * (len(extent) - 1 - axis_at))
    return factor_of


def deal_out(key, own, number, rows, number_of, top, reach, skew):
    sequence = jax.random.permutation(key, number_of)
    heavy_load, usual = portions_of(number_of, rows * top, reach, skew, True), portions_of(number_of, rows * top, reach, skew, False)
    places = jnp.arange(number_of)

    def named(sizes, offset_by):
        used = int((sizes > 0).sum())
        fixed = max(1, used // 4)
        moved = fixed + (places - fixed + offset_by * (used - fixed)) % max(1, number_of - fixed)
        return jnp.zeros((number_of,), jnp.int32).at[sequence[jnp.where(places < fixed, places, moved)]].set(jnp.asarray(sizes, jnp.int32))

    sizes = jnp.where(number % 4 == 0, named(heavy_load, number // 4), named(usual, number - number // 4 - 1))
    mixed = jax.random.permutation(jax.random.fold_in(own, 3), number_of)
    giver, taker = mixed[0:number_of // 2 * 2:2], mixed[1:number_of // 2 * 2:2]
    margin = jnp.minimum(sizes[giver] - 1, reach - sizes[taker]) // 2
    margin = jnp.where((giver == sequence[0]) | (taker == sequence[0]) | (sizes[taker] == 0), 0, jnp.maximum(margin, 0))
    moved = jax.random.randint(jax.random.fold_in(own, 4), (number_of // 2,), 0, 1 << 20) % (margin + 1)
    sizes = sizes.at[giver].add(-moved).at[taker].add(moved)
    members = jnp.searchsorted(jnp.cumsum(sizes), jnp.arange(rows * top), side="right").astype(jnp.int32)
    table = members.reshape(top, rows).T
    table = table[jax.random.permutation(jax.random.fold_in(own, 1), rows)]
    offset_by = jax.random.randint(jax.random.fold_in(own, 2), (rows, 1), 0, top)
    return jnp.take_along_axis(table, (jnp.arange(top)[None, :] + offset_by) % top, axis=1)


def portions_of(amount, total, bound, slope, full):
    portions = [(1 << 20) // math.isqrt(grade ** slope) + 1 for grade in range(1, amount + 1)]
    largest = bound if full else min(bound, max(-(-total // amount), total * portions[0] // sum(portions)))
    least = 1 if total - largest >= amount - 1 else 0
    counts, spare = [largest] + [least] * (amount - 1), total - largest - least * (amount - 1)
    while spare > 0:
        candidates = [i for i in range(1, amount) if counts[i] < largest] or [i for i in range(1, amount) if counts[i] < bound]
        mass, remaining = sum([portions[i] for i in candidates]), spare
        for i in candidates:
            more = min(bound - counts[i], max(1, remaining * portions[i] // mass), spare)
            counts[i] = counts[i] + more
            spare = spare - more
    return np.array(counts)


def noise(own_key, dims, scale, most, split=(), held_as=jnp.bfloat16):
    gain = steps_of(own_key, dims, split, -0.22, 0.18) if split else 1.0
    drawn = jax.random.normal(own_key, dims, jnp.float32) * scale * gain
    return jnp.minimum(jnp.maximum(drawn, -most), most).astype(held_as)


def setup_inputs(seed: int = 0) -> dict:
    streams_of = jax.random.split(jax.random.key(seed), 13)
    slave_basis = noise(streams_of[0], (SBLOCKS, NODES, QPTS), 0.25, 1.5, ((0, 16),))
    master_basis = noise(streams_of[1], (MBLOCKS, NODES, QPTS), 0.25, 1.5, ((0, 128),))
    slave_gap = noise(streams_of[2], (SBLOCKS, NODES), 1.0, 6.0, ((0, 16),), jnp.float32)
    master_disp = noise(streams_of[3], (MBLOCKS, NODES), 1.0, 6.0, ((0, 128),), jnp.float32)
    pressure = noise(streams_of[4], (SBLOCKS, NODES), 1.0, 6.0, ((0, 16),), jnp.float32)
    active = plant((jax.random.randint(streams_of[5], (SBLOCKS, NODES), 0, 3) < 2).astype(jnp.int32), jax.random.fold_in(streams_of[5], 1), 0, 1)
    need_owner_keys = jax.random.split(jax.random.fold_in(streams_of[6], 1), NEEDS // NEED_DEV)
    need_owner_turns = jax.random.permutation(jax.random.fold_in(streams_of[6], 3), NEEDS // NEED_DEV)
    need_owner = jax.vmap(lambda own, number: deal_out(jax.random.fold_in(streams_of[6], 2), own, number, NEED_DEV, N_SLAVE * N_MASTER, 1, CAP, 2))(need_owner_keys, need_owner_turns).reshape((NEEDS, 1))
    need_slot = plant(jax.random.randint(streams_of[7], (NEEDS,), 0, MB_DEV), jax.random.fold_in(streams_of[7], 1), 0, MB_DEV - 1).astype(jnp.int32)
    pair_need = plant(jax.random.randint(streams_of[8], (PAIRS,), 0, NEED_DEV), jax.random.fold_in(streams_of[8], 1), 0, NEED_DEV - 1).astype(jnp.int32)
    pair_slave = plant(jax.random.randint(streams_of[9], (PAIRS,), 0, SB_DEV), jax.random.fold_in(streams_of[9], 1), 0, SB_DEV - 1).astype(jnp.int32)
    pair_segs = plant(jax.random.randint(streams_of[10], (PAIRS,), 1, SEGS + 1), jax.random.fold_in(streams_of[10], 1), 1, SEGS).astype(jnp.int32)
    pair_weight = jnp.clip(jnp.exp(math.log(0.5) - 2.3025851 * jax.random.uniform(streams_of[11], (PAIRS, QPTS), jnp.float32) ** steps_of(streams_of[11], (PAIRS, QPTS), ((0, 128),), -0.2, 0.2)), 0.05, 0.5)
    return dict(slave_basis=slave_basis, master_basis=master_basis, slave_gap=slave_gap, master_disp=master_disp, pressure=pressure, active=active, need_owner=need_owner, need_slot=need_slot, pair_need=pair_need, pair_slave=pair_slave, pair_segs=pair_segs, pair_weight=pair_weight)


def reference(slave_basis, master_basis, slave_gap, master_disp, pressure, active, need_owner, need_slot, pair_need, pair_slave, pair_segs, pair_weight):
    high = lax.Precision.HIGHEST
    device_of = (jnp.arange(PAIRS, dtype=jnp.int32) // PAIR_DEV).astype(jnp.int32)
    slave_global = (device_of // N_MASTER * SB_DEV + pair_slave).astype(jnp.int32)
    need_global = (device_of * NEED_DEV + pair_need).astype(jnp.int32)
    master_global = (need_owner[need_global, 0] * MB_DEV + need_slot[need_global]).astype(jnp.int32)
    limit = GAUSS * pair_segs
    weights = jnp.where(jnp.arange(QPTS, dtype=jnp.int32)[None, :] < limit[:, None], pair_weight, jnp.zeros_like(pair_weight))
    slave_weight = jax.ops.segment_sum(weights, slave_global, num_segments=SBLOCKS)
    slave_float = slave_basis.astype(jnp.float32)
    master_float = master_basis.astype(jnp.float32)
    squares = jnp.square(slave_float)
    lump = 1.0 + jnp.einsum('snq,sq->sn', squares, slave_weight, precision=high)
    root_lump = jnp.sqrt(lump)
    blocks = PAIRS // PAIR_DEV

    def tiles_for(index):
        start = (index * PAIR_DEV).astype(jnp.int32)
        sg = lax.dynamic_slice_in_dim(slave_global, start, PAIR_DEV)
        mg = lax.dynamic_slice_in_dim(master_global, start, PAIR_DEV)
        wt = lax.dynamic_slice_in_dim(weights, start, PAIR_DEV)
        left = slave_basis[sg].astype(jnp.float32)
        scaled = (master_basis[mg].astype(jnp.float32) * wt[:, None, :]).astype(jnp.bfloat16)
        tile = jnp.einsum('pnq,pmq->pnm', left, scaled.astype(jnp.float32), precision=high)
        return tile.astype(jnp.bfloat16)
    stored = lax.map(tiles_for, jnp.arange(blocks, dtype=jnp.int32))
    tile_out = stored.reshape(PAIRS, NODES, NODES)

    def coupled_sum(disp):
        proj = jnp.einsum('mnq,mn->mq', master_float, disp, precision=high)
        pair_terms = weights * proj[master_global]
        summed = jax.ops.segment_sum(pair_terms, slave_global, num_segments=SBLOCKS)
        return jnp.einsum('snq,sq->sn', slave_float, summed, precision=high)

    def force_sum(lam):
        slave_proj = jnp.einsum('snq,sn->sq', slave_float, lam, precision=high)
        pair_terms = weights * slave_proj[slave_global]
        loads = jax.ops.segment_sum(pair_terms, master_global, num_segments=MBLOCKS)
        return jnp.einsum('mnq,mq->mn', master_float, loads, precision=high)
    lam = pressure
    disp = master_disp
    flags = active == 1
    for update in range(ITERS):
        gap = slave_gap - coupled_sum(disp) / root_lump
        lam = jnp.where(flags, lam - 1.0 * gap, jnp.zeros_like(lam))
        disp = disp - 0.05 * force_sum(lam)
    return (lam, disp, tile_out)
```

```python
import functools

import jax
import jax.numpy as jnp
from jax import lax
from jax.experimental import pallas as pl
from jax.experimental.pallas import tpu as pltpu
from jax.sharding import PartitionSpec as P

GAUSS = 16
ITERS = 2
GROUP = 32


def tile_kernel(group, sidx_ref, nidx_ref, slave_ref, recv_ref, w_ref, out_ref):
    base = pl.program_id(0) * group

    def body(g, carry):
        s = sidx_ref[base + g]
        r = nidx_ref[base + g]
        left = slave_ref[s]
        w = w_ref[pl.ds(g, 1), :]
        right = (recv_ref[r].astype(jnp.float32) * w).astype(jnp.bfloat16)
        tile = lax.dot_general(
            left, right, (((1,), (1,)), ((), ())), preferred_element_type=jnp.float32
        )
        out_ref[g] = tile.astype(out_ref.dtype)
        return carry

    lax.fori_loop(0, group, body, 0)


def build_tiles(slave_basis, received, pair_slave, pair_need, weights):
    pairs = weights.shape[0]
    nodes, qpts = slave_basis.shape[1], slave_basis.shape[2]
    group = GROUP
    grid_spec = pltpu.PrefetchScalarGridSpec(
        num_scalar_prefetch=2,
        grid=(pairs // group,),
        in_specs=[
            pl.BlockSpec(slave_basis.shape, lambda i, s, n: (0, 0, 0)),
            pl.BlockSpec(received.shape, lambda i, s, n: (0, 0, 0)),
            pl.BlockSpec((group, qpts), lambda i, s, n: (i, 0)),
        ],
        out_specs=pl.BlockSpec((group, nodes, nodes), lambda i, s, n: (i, 0, 0)),
    )
    return pl.pallas_call(
        functools.partial(tile_kernel, group),
        grid_spec=grid_spec,
        out_shape=jax.ShapeDtypeStruct((pairs, nodes, nodes), jnp.bfloat16),
        compiler_params=pltpu.CompilerParams(vmem_limit_bytes=48 * 1024 * 1024),
    )(pair_slave, pair_need, slave_basis, received, weights)


def on_device(
    slave_basis,
    master_basis,
    slave_gap,
    master_disp,
    pressure,
    active,
    need_owner,
    need_slot,
    pair_need,
    pair_slave,
    pair_segs,
    pair_weight,
):
    high = lax.Precision.HIGHEST
    everyone = ("slave", "master")
    mb_dev = master_basis.shape[0]
    need_dev = need_slot.shape[0]
    qpts = slave_basis.shape[2]
    request = need_owner[:, 0] * mb_dev + need_slot
    every_basis = lax.all_gather(master_basis, everyone, axis=0, tiled=True)
    mblocks = every_basis.shape[0]
    received = every_basis[request]
    limit = GAUSS * pair_segs
    weights = jnp.where(
        jnp.arange(qpts, dtype=jnp.int32)[None, :] < limit[:, None],
        pair_weight,
        jnp.zeros_like(pair_weight),
    )
    slave_count = slave_basis.shape[0]
    slave_onehot = (
        pair_slave[None, :] == jnp.arange(slave_count, dtype=jnp.int32)[:, None]
    ).astype(jnp.float32)
    need_onehot = (pair_need[None, :] == jnp.arange(need_dev, dtype=jnp.int32)[:, None]).astype(
        jnp.float32
    )
    block_onehot = (request[None, :] == jnp.arange(mblocks, dtype=jnp.int32)[:, None]).astype(
        jnp.float32
    )
    slave_weight = jnp.dot(slave_onehot, weights, precision=high)
    slave_float = slave_basis.astype(jnp.float32)
    master_float = master_basis.astype(jnp.float32)
    squares = jnp.square(slave_float)
    lump_part = jnp.einsum("snq,sq->sn", squares, slave_weight, precision=high)

    stored = build_tiles(slave_basis, received, pair_slave, pair_need, weights)
    lam = pressure
    disp = master_disp
    flags = active == 1
    root_lump = None
    for update in range(ITERS):
        own_proj = jnp.einsum("mnq,mn->mq", master_float, disp, precision=high)
        every_proj = lax.all_gather(own_proj, everyone, axis=0, tiled=True)
        need_proj = every_proj[request]
        pair_terms = weights * need_proj[pair_need]
        slave_terms = jnp.dot(slave_onehot, pair_terms, precision=high)
        partial_coupled = jnp.einsum("snq,sq->sn", slave_float, slave_terms, precision=high)
        if update == 0:
            lump_total, coupled = lax.psum((lump_part, partial_coupled), "master")
            root_lump = jnp.sqrt(1.0 + lump_total)
        else:
            coupled = lax.psum(partial_coupled, "master")
        gap = slave_gap - coupled / root_lump
        lam = jnp.where(flags, lam - 1.0 * gap, jnp.zeros_like(lam))
        slave_proj = jnp.einsum("snq,sn->sq", slave_float, lam, precision=high)
        need_load = jnp.dot(need_onehot, weights * slave_proj[pair_slave], precision=high)
        block_load = jnp.dot(block_onehot, need_load, precision=high)
        own_load = lax.psum_scatter(block_load, everyone, scatter_dimension=0, tiled=True)
        force = jnp.einsum("mnq,mq->mn", master_float, own_load, precision=high)
        disp = disp - 0.05 * force
    return (lam, disp, stored)


def solution(mesh):
    return jax.shard_map(
        on_device,
        mesh=mesh,
        in_specs=(
            P("slave", None, None),
            P(("slave", "master"), None, None),
            P("slave", None),
            P(("slave", "master"), None),
            P("slave", None),
            P("slave", None),
            P(("slave", "master"), None),
            P(("slave", "master")),
            P(("slave", "master")),
            P(("slave", "master")),
            P(("slave", "master")),
            P(("slave", "master"), None),
        ),
        out_specs=(
            P("slave", None),
            P(("slave", "master"), None),
            P(("slave", "master"), None, None),
        ),
        check_vma=False,
    )
```

```python
import functools

import jax
import jax.numpy as jnp
from jax import lax
from jax.experimental import pallas as pl
from jax.experimental.pallas import tpu as pltpu
from jax.sharding import PartitionSpec as P

GAUSS = 16
ITERS = 2
GROUP = 64


def tile_kernel(group, sidx_ref, nidx_ref, mreq_ref, slave_ref, basis_hbm, w_ref, out_ref, recv, sems):
    need = recv.shape[0]

    @pl.when(pl.program_id(0) == 0)
    def _():
        for r in range(need):
            pltpu.make_async_copy(basis_hbm.at[mreq_ref[r]], recv.at[r], sems.at[r]).start()
        for r in range(need):
            pltpu.make_async_copy(basis_hbm.at[0], recv.at[r], sems.at[r]).wait()

    base = pl.program_id(0) * group
    for g in range(group):
        s = sidx_ref[base + g]
        r = nidx_ref[base + g]
        left = slave_ref[s]
        w = w_ref[pl.ds(g, 1), :]
        right = (recv[r].astype(jnp.float32) * w).astype(jnp.bfloat16)
        tile = lax.dot_general(
            left, right, (((1,), (1,)), ((), ())), preferred_element_type=jnp.float32
        )
        out_ref[g] = tile.astype(out_ref.dtype)


def build_tiles(slave_basis, every_basis, request, pair_slave, pair_need, weights):
    pairs = weights.shape[0]
    nodes, qpts = slave_basis.shape[1], slave_basis.shape[2]
    need = request.shape[0]
    group = GROUP
    grid_spec = pltpu.PrefetchScalarGridSpec(
        num_scalar_prefetch=3,
        grid=(pairs // group,),
        in_specs=[
            pl.BlockSpec(slave_basis.shape, lambda i, s, n, m: (0, 0, 0)),
            pl.BlockSpec(memory_space=pl.ANY),
            pl.BlockSpec((group, qpts), lambda i, s, n, m: (i, 0)),
        ],
        out_specs=pl.BlockSpec((group, nodes, nodes), lambda i, s, n, m: (i, 0, 0)),
        scratch_shapes=[
            pltpu.VMEM((need, nodes, qpts), jnp.bfloat16),
            pltpu.SemaphoreType.DMA((need,)),
        ],
    )
    return pl.pallas_call(
        functools.partial(tile_kernel, group),
        grid_spec=grid_spec,
        out_shape=jax.ShapeDtypeStruct((pairs, nodes, nodes), jnp.bfloat16),
        compiler_params=pltpu.CompilerParams(
            vmem_limit_bytes=48 * 1024 * 1024, dimension_semantics=("arbitrary",)
        ),
    )(pair_slave, pair_need, request, slave_basis, every_basis, weights)


def master_sum(x):
    count = lax.axis_size("master")
    spread = jnp.broadcast_to(x[None], (count,) + x.shape)
    got = lax.all_to_all(spread, "master", split_axis=0, concat_axis=0, tiled=True)
    return jnp.sum(got, axis=0)


def on_device(
    slave_basis,
    master_basis,
    slave_gap,
    master_disp,
    pressure,
    active,
    need_owner,
    need_slot,
    pair_need,
    pair_slave,
    pair_segs,
    pair_weight,
):
    high = lax.Precision.HIGHEST
    everyone = ("slave", "master")
    peers = lax.axis_size(everyone)
    mb_dev = master_basis.shape[0]
    need_dev = need_slot.shape[0]
    cap = 2 * need_dev // peers
    qpts = slave_basis.shape[2]
    owner = need_owner[:, 0]
    request = owner * mb_dev + need_slot
    every_basis = lax.all_gather(master_basis, everyone, axis=0, tiled=True)

    match = (owner[:, None] == jnp.arange(peers, dtype=jnp.int32)[None, :]).astype(jnp.int32)
    earlier = jnp.cumsum(match, axis=0) - match
    rank = jnp.sum(earlier * match, axis=1)
    position = owner * cap + rank
    slots = jnp.zeros((peers * cap,), jnp.int32).at[position].set(need_slot)
    filled = jnp.zeros((peers * cap,), jnp.int32).at[position].set(1)
    asked = lax.all_to_all(
        jnp.stack([slots, filled]).reshape(2, peers, cap),
        everyone,
        split_axis=1,
        concat_axis=1,
        tiled=True,
    )
    wanted = asked[0].reshape(-1)
    present = asked[1].reshape(-1)

    limit = GAUSS * pair_segs
    weights = jnp.where(
        jnp.arange(qpts, dtype=jnp.int32)[None, :] < limit[:, None],
        pair_weight,
        jnp.zeros_like(pair_weight),
    )
    slave_count = slave_basis.shape[0]
    slave_onehot = (
        pair_slave[None, :] == jnp.arange(slave_count, dtype=jnp.int32)[:, None]
    ).astype(jnp.float32)
    need_onehot = (pair_need[None, :] == jnp.arange(need_dev, dtype=jnp.int32)[:, None]).astype(
        jnp.float32
    )
    owner_onehot = (
        (wanted[None, :] == jnp.arange(mb_dev, dtype=jnp.int32)[:, None]) & (present[None, :] == 1)
    ).astype(jnp.float32)
    slave_weight = jnp.dot(slave_onehot, weights, precision=high)
    slave_float = slave_basis.astype(jnp.float32)
    master_float = master_basis.astype(jnp.float32)
    squares = jnp.square(slave_float)
    lump_part = jnp.einsum("snq,sq->sn", squares, slave_weight, precision=high)

    stored = build_tiles(slave_basis, every_basis, request, pair_slave, pair_need, weights)
    lam = pressure
    disp = master_disp
    flags = active == 1
    root_lump = None
    for update in range(ITERS):
        own_proj = jnp.einsum("mnq,mn->mq", master_float, disp, precision=high)
        outgoing_proj = own_proj[wanted].reshape(peers, cap, qpts)
        returned = lax.all_to_all(outgoing_proj, everyone, split_axis=0, concat_axis=0, tiled=True)
        need_proj = returned.reshape(peers * cap, qpts)[position]
        pair_terms = weights * need_proj[pair_need]
        slave_terms = jnp.dot(slave_onehot, pair_terms, precision=high)
        partial_coupled = jnp.einsum("snq,sq->sn", slave_float, slave_terms, precision=high)
        if update == 0:
            both = master_sum(jnp.stack([lump_part, partial_coupled]))
            root_lump = jnp.sqrt(1.0 + both[0])
            coupled = both[1]
        else:
            coupled = master_sum(partial_coupled)
        gap = slave_gap - coupled / root_lump
        lam = jnp.where(flags, lam - 1.0 * gap, jnp.zeros_like(lam))
        slave_proj = jnp.einsum("snq,sn->sq", slave_float, lam, precision=high)
        need_load = jnp.dot(need_onehot, weights * slave_proj[pair_slave], precision=high)
        outbound = jnp.zeros((peers * cap, qpts), jnp.float32).at[position].set(need_load)
        inbound = lax.all_to_all(
            outbound.reshape(peers, cap, qpts), everyone, split_axis=0, concat_axis=0, tiled=True
        )
        own_load = jnp.dot(owner_onehot, inbound.reshape(peers * cap, qpts), precision=high)
        force = jnp.einsum("mnq,mq->mn", master_float, own_load, precision=high)
        disp = disp - 0.05 * force
    return (lam, disp, stored)


def solution(mesh):
    return jax.shard_map(
        on_device,
        mesh=mesh,
        in_specs=(
            P("slave", None, None),
            P(("slave", "master"), None, None),
            P("slave", None),
            P(("slave", "master"), None),
            P("slave", None),
            P("slave", None),
            P(("slave", "master"), None),
            P(("slave", "master")),
            P(("slave", "master")),
            P(("slave", "master")),
            P(("slave", "master")),
            P(("slave", "master"), None),
        ),
        out_specs=(
            P("slave", None),
            P(("slave", "master"), None),
            P(("slave", "master"), None, None),
        ),
        check_vma=False,
    )
```

```python
import functools

import jax
import jax.numpy as jnp
from jax import lax
from jax.experimental import pallas as pl
from jax.experimental.pallas import tpu as pltpu
from jax.sharding import PartitionSpec as P

GAUSS = 16
ITERS = 2
GROUP = 64


def tile_kernel(group, sidx_ref, nidx_ref, mreq_ref, slave_ref, basis_hbm, w_ref, out_ref, recv, sems):
    need = recv.shape[0]

    @pl.when(pl.program_id(0) == 0)
    def _():
        for r in range(need):
            pltpu.make_async_copy(basis_hbm.at[mreq_ref[r]], recv.at[r], sems.at[r]).start()
        for r in range(need):
            pltpu.make_async_copy(basis_hbm.at[0], recv.at[r], sems.at[r]).wait()

    base = pl.program_id(0) * group
    for g in range(group):
        s = sidx_ref[base + g]
        r = nidx_ref[base + g]
        left = slave_ref[s]
        w = w_ref[pl.ds(g, 1), :]
        right = (recv[r].astype(jnp.float32) * w).astype(jnp.bfloat16)
        tile = lax.dot_general(
            left, right, (((1,), (1,)), ((), ())), preferred_element_type=jnp.float32
        )
        out_ref[g] = tile.astype(out_ref.dtype)


def build_tiles(slave_basis, every_basis, request, pair_slave, pair_need, weights):
    pairs = weights.shape[0]
    nodes, qpts = slave_basis.shape[1], slave_basis.shape[2]
    need = request.shape[0]
    group = GROUP
    grid_spec = pltpu.PrefetchScalarGridSpec(
        num_scalar_prefetch=3,
        grid=(pairs // group,),
        in_specs=[
            pl.BlockSpec(slave_basis.shape, lambda i, s, n, m: (0, 0, 0)),
            pl.BlockSpec(memory_space=pl.ANY),
            pl.BlockSpec((group, qpts), lambda i, s, n, m: (i, 0)),
        ],
        out_specs=pl.BlockSpec((group, nodes, nodes), lambda i, s, n, m: (i, 0, 0)),
        scratch_shapes=[
            pltpu.VMEM((need, nodes, qpts), jnp.bfloat16),
            pltpu.SemaphoreType.DMA((need,)),
        ],
    )
    cost = pl.CostEstimate(
        flops=2 * pairs * nodes * nodes * qpts,
        bytes_accessed=pairs * nodes * nodes * 2 + need * nodes * qpts * 2 + pairs * qpts * 4,
        transcendentals=0,
    )
    return pl.pallas_call(
        functools.partial(tile_kernel, group),
        grid_spec=grid_spec,
        out_shape=jax.ShapeDtypeStruct((pairs, nodes, nodes), jnp.bfloat16),
        compiler_params=pltpu.CompilerParams(
            vmem_limit_bytes=48 * 1024 * 1024, dimension_semantics=("arbitrary",)
        ),
        cost_estimate=cost,
    )(pair_slave, pair_need, request, slave_basis, every_basis, weights)


def master_sum(x):
    count = lax.axis_size("master")
    spread = jnp.broadcast_to(x[None], (count,) + x.shape)
    got = lax.all_to_all(spread, "master", split_axis=0, concat_axis=0, tiled=True)
    return jnp.sum(got, axis=0)


def on_device(
    slave_basis,
    master_basis,
    slave_gap,
    master_disp,
    pressure,
    active,
    need_owner,
    need_slot,
    pair_need,
    pair_slave,
    pair_segs,
    pair_weight,
):
    high = lax.Precision.HIGHEST
    everyone = ("slave", "master")
    peers = lax.axis_size(everyone)
    mb_dev = master_basis.shape[0]
    need_dev = need_slot.shape[0]
    qpts = slave_basis.shape[2]
    owner = need_owner[:, 0]
    request = owner * mb_dev + need_slot
    every_basis = lax.all_gather(master_basis, everyone, axis=0, tiled=True)

    limit = GAUSS * pair_segs
    weights = jnp.where(
        jnp.arange(qpts, dtype=jnp.int32)[None, :] < limit[:, None],
        pair_weight,
        jnp.zeros_like(pair_weight),
    )
    slave_count = slave_basis.shape[0]
    slave_onehot = (
        pair_slave[None, :] == jnp.arange(slave_count, dtype=jnp.int32)[:, None]
    ).astype(jnp.float32)
    need_onehot = (pair_need[None, :] == jnp.arange(need_dev, dtype=jnp.int32)[:, None]).astype(
        jnp.float32
    )
    mblocks = peers * mb_dev
    block_onehot = (request[None, :] == jnp.arange(mblocks, dtype=jnp.int32)[:, None]).astype(
        jnp.float32
    )
    slave_weight = jnp.dot(slave_onehot, weights, precision=high)
    slave_float = slave_basis.astype(jnp.float32)
    master_float = master_basis.astype(jnp.float32)
    squares = jnp.square(slave_float)
    lump_part = jnp.einsum("snq,sq->sn", squares, slave_weight, precision=high)

    stored = build_tiles(slave_basis, every_basis, request, pair_slave, pair_need, weights)
    lam = pressure
    disp = master_disp
    flags = active == 1
    root_lump = None
    for update in range(ITERS):
        own_proj = jnp.einsum("mnq,mn->mq", master_float, disp, precision=high)
        outgoing_proj = jnp.broadcast_to(own_proj[None], (peers,) + own_proj.shape)
        returned = lax.all_to_all(outgoing_proj, everyone, split_axis=0, concat_axis=0, tiled=True)
        need_proj = returned.reshape(mblocks, qpts)[request]
        pair_terms = weights * need_proj[pair_need]
        slave_terms = jnp.dot(slave_onehot, pair_terms, precision=high)
        partial_coupled = jnp.einsum("snq,sq->sn", slave_float, slave_terms, precision=high)
        if update == 0:
            both = master_sum(jnp.stack([lump_part, partial_coupled]))
            root_lump = jnp.sqrt(1.0 + both[0])
            coupled = both[1]
        else:
            coupled = master_sum(partial_coupled)
        gap = slave_gap - coupled / root_lump
        lam = jnp.where(flags, lam - 1.0 * gap, jnp.zeros_like(lam))
        slave_proj = jnp.einsum("snq,sn->sq", slave_float, lam, precision=high)
        need_load = jnp.dot(need_onehot, weights * slave_proj[pair_slave], precision=high)
        outbound = jnp.dot(block_onehot, need_load, precision=high)
        inbound = lax.all_to_all(
            outbound.reshape(peers, mb_dev, qpts), everyone, split_axis=0, concat_axis=0, tiled=True
        )
        own_load = jnp.sum(inbound, axis=0)
        force = jnp.einsum("mnq,mq->mn", master_float, own_load, precision=high)
        disp = disp - 0.05 * force
    return (lam, disp, stored)


def solution(mesh):
    return jax.shard_map(
        on_device,
        mesh=mesh,
        in_specs=(
            P("slave", None, None),
            P(("slave", "master"), None, None),
            P("slave", None),
            P(("slave", "master"), None),
            P("slave", None),
            P("slave", None),
            P(("slave", "master"), None),
            P(("slave", "master")),
            P(("slave", "master")),
            P(("slave", "master")),
            P(("slave", "master")),
            P(("slave", "master"), None),
        ),
        out_specs=(
            P("slave", None),
            P(("slave", "master"), None),
            P(("slave", "master"), None, None),
        ),
        check_vma=False,
    )
```

```python
import functools

import jax
import jax.numpy as jnp
from jax import lax
from jax.experimental import pallas as pl
from jax.experimental.pallas import tpu as pltpu
from jax.sharding import PartitionSpec as P

GAUSS = 16
ITERS = 2
GROUP = 64


def tile_kernel(group, sidx_ref, nidx_ref, mreq_ref, slave_ref, basis_hbm, w_ref, out_ref, recv, sems):
    need = recv.shape[0]

    @pl.when(pl.program_id(0) == 0)
    def _():
        for r in range(need):
            pltpu.make_async_copy(basis_hbm.at[mreq_ref[r]], recv.at[r], sems.at[r]).start()
        for r in range(need):
            pltpu.make_async_copy(basis_hbm.at[0], recv.at[r], sems.at[r]).wait()

    base = pl.program_id(0) * group
    for g in range(group):
        s = sidx_ref[base + g]
        r = nidx_ref[base + g]
        left = slave_ref[s]
        w = w_ref[pl.ds(g, 1), :]
        right = (recv[r].astype(jnp.float32) * w).astype(jnp.bfloat16)
        tile = lax.dot_general(
            left, right, (((1,), (1,)), ((), ())), preferred_element_type=jnp.float32
        )
        out_ref[g] = tile.astype(out_ref.dtype)


def build_tiles(slave_basis, every_basis, request, pair_slave, pair_need, weights):
    pairs = weights.shape[0]
    nodes, qpts = slave_basis.shape[1], slave_basis.shape[2]
    need = request.shape[0]
    group = GROUP
    grid_spec = pltpu.PrefetchScalarGridSpec(
        num_scalar_prefetch=3,
        grid=(pairs // group,),
        in_specs=[
            pl.BlockSpec(slave_basis.shape, lambda i, s, n, m: (0, 0, 0)),
            pl.BlockSpec(memory_space=pl.ANY),
            pl.BlockSpec((group, qpts), lambda i, s, n, m: (i, 0)),
        ],
        out_specs=pl.BlockSpec((group, nodes, nodes), lambda i, s, n, m: (i, 0, 0)),
        scratch_shapes=[
            pltpu.VMEM((need, nodes, qpts), jnp.bfloat16),
            pltpu.SemaphoreType.DMA((need,)),
        ],
    )
    cost = pl.CostEstimate(
        flops=2 * pairs * nodes * nodes * qpts,
        bytes_accessed=pairs * nodes * nodes * 2 + need * nodes * qpts * 2 + pairs * qpts * 4,
        transcendentals=0,
    )
    return pl.pallas_call(
        functools.partial(tile_kernel, group),
        grid_spec=grid_spec,
        out_shape=jax.ShapeDtypeStruct((pairs, nodes, nodes), jnp.bfloat16),
        compiler_params=pltpu.CompilerParams(
            vmem_limit_bytes=48 * 1024 * 1024, dimension_semantics=("arbitrary",)
        ),
        cost_estimate=cost,
    )(pair_slave, pair_need, request, slave_basis, every_basis, weights)


def exchange_kernel(axes, sizes, spread, x_ref, o_ref, landed, send_sems, recv_sems):
    n = 1
    for s in sizes:
        n *= s
    me = 0
    for a, s in zip(axes, sizes):
        me = me * s + lax.axis_index(a)

    def device_of(t):
        coords = {}
        for a, s in zip(reversed(axes), reversed(sizes)):
            coords[a] = t % s
            t = t // s
        return tuple(coords[a] if a in coords else lax.axis_index(a) for a in ("slave", "master"))

    def source(t):
        return x_ref if spread else x_ref.at[t]

    def start(k, carry):
        t = lax.rem(me + k, n)
        pltpu.make_async_remote_copy(
            src_ref=source(t), dst_ref=landed.at[me], send_sem=send_sems.at[t],
            recv_sem=recv_sems.at[me], device_id=device_of(t),
            device_id_type=pl.DeviceIdType.MESH,
        ).start()
        return carry

    lax.fori_loop(1, n, start, 0)
    own = x_ref[...] if spread else x_ref[me]
    o_ref[me] = own

    def finish(k, carry):
        t = lax.rem(me + k, n)
        f = lax.rem(me + n - k, n)
        pltpu.make_async_remote_copy(
            src_ref=source(t), dst_ref=landed.at[me], send_sem=send_sems.at[t],
            recv_sem=recv_sems.at[me], device_id=device_of(t),
            device_id_type=pl.DeviceIdType.MESH,
        ).wait_send()
        pltpu.make_async_remote_copy(
            src_ref=source(f), dst_ref=landed.at[f], send_sem=send_sems.at[f],
            recv_sem=recv_sems.at[f], device_id=device_of(f),
            device_id_type=pl.DeviceIdType.MESH,
        ).wait_recv()
        o_ref[f] = landed[f]
        return carry

    lax.fori_loop(1, n, finish, 0)


def exchange(x, axes, sizes, spread):
    n = 1
    for s in sizes:
        n *= s
    piece = x.shape if spread else x.shape[1:]
    return pl.pallas_call(
        functools.partial(exchange_kernel, axes, sizes, spread),
        out_shape=jax.ShapeDtypeStruct((n,) + piece, x.dtype),
        in_specs=[pl.BlockSpec(memory_space=pltpu.VMEM)],
        out_specs=pl.BlockSpec(memory_space=pltpu.VMEM),
        scratch_shapes=[
            pltpu.VMEM((n,) + piece, x.dtype),
            pltpu.SemaphoreType.DMA((n,)),
            pltpu.SemaphoreType.DMA((n,)),
        ],
        compiler_params=pltpu.CompilerParams(has_side_effects=True),
    )(x)


def master_sum(x):
    count = lax.axis_size("master")
    got = exchange(x, ("master",), (count,), True)
    return jnp.sum(got, axis=0)


def on_device(
    slave_basis,
    master_basis,
    slave_gap,
    master_disp,
    pressure,
    active,
    need_owner,
    need_slot,
    pair_need,
    pair_slave,
    pair_segs,
    pair_weight,
):
    high = lax.Precision.HIGHEST
    everyone = ("slave", "master")
    peers = lax.axis_size(everyone)
    sizes = (lax.axis_size("slave"), lax.axis_size("master"))
    mb_dev = master_basis.shape[0]
    need_dev = need_slot.shape[0]
    qpts = slave_basis.shape[2]
    owner = need_owner[:, 0]
    request = owner * mb_dev + need_slot
    every_basis = lax.all_gather(master_basis, everyone, axis=0, tiled=True)

    limit = GAUSS * pair_segs
    weights = jnp.where(
        jnp.arange(qpts, dtype=jnp.int32)[None, :] < limit[:, None],
        pair_weight,
        jnp.zeros_like(pair_weight),
    )
    slave_count = slave_basis.shape[0]
    slave_onehot = (
        pair_slave[None, :] == jnp.arange(slave_count, dtype=jnp.int32)[:, None]
    ).astype(jnp.float32)
    need_onehot = (pair_need[None, :] == jnp.arange(need_dev, dtype=jnp.int32)[:, None]).astype(
        jnp.float32
    )
    mblocks = peers * mb_dev
    block_onehot = (request[None, :] == jnp.arange(mblocks, dtype=jnp.int32)[:, None]).astype(
        jnp.float32
    )
    slave_weight = jnp.dot(slave_onehot, weights, precision=high)
    slave_float = slave_basis.astype(jnp.float32)
    master_float = master_basis.astype(jnp.float32)
    squares = jnp.square(slave_float)
    lump_part = jnp.einsum("snq,sq->sn", squares, slave_weight, precision=high)

    stored = build_tiles(slave_basis, every_basis, request, pair_slave, pair_need, weights)
    lam = pressure
    disp = master_disp
    flags = active == 1
    root_lump = None
    for update in range(ITERS):
        own_proj = jnp.einsum("mnq,mn->mq", master_float, disp, precision=high)
        returned = exchange(own_proj, everyone, sizes, True)
        need_proj = returned.reshape(mblocks, qpts)[request]
        pair_terms = weights * need_proj[pair_need]
        slave_terms = jnp.dot(slave_onehot, pair_terms, precision=high)
        partial_coupled = jnp.einsum("snq,sq->sn", slave_float, slave_terms, precision=high)
        if update == 0:
            both = master_sum(jnp.stack([lump_part, partial_coupled]))
            root_lump = jnp.sqrt(1.0 + both[0])
            coupled = both[1]
        else:
            coupled = master_sum(partial_coupled)
        gap = slave_gap - coupled / root_lump
        lam = jnp.where(flags, lam - 1.0 * gap, jnp.zeros_like(lam))
        slave_proj = jnp.einsum("snq,sn->sq", slave_float, lam, precision=high)
        need_load = jnp.dot(need_onehot, weights * slave_proj[pair_slave], precision=high)
        outbound = jnp.dot(block_onehot, need_load, precision=high)
        inbound = exchange(outbound.reshape(peers, mb_dev, qpts), everyone, sizes, False)
        own_load = jnp.sum(inbound, axis=0)
        force = jnp.einsum("mnq,mq->mn", master_float, own_load, precision=high)
        disp = disp - 0.05 * force
    return (lam, disp, stored)


def solution(mesh):
    return jax.shard_map(
        on_device,
        mesh=mesh,
        in_specs=(
            P("slave", None, None),
            P(("slave", "master"), None, None),
            P("slave", None),
            P(("slave", "master"), None),
            P("slave", None),
            P("slave", None),
            P(("slave", "master"), None),
            P(("slave", "master")),
            P(("slave", "master")),
            P(("slave", "master")),
            P(("slave", "master")),
            P(("slave", "master"), None),
        ),
        out_specs=(
            P("slave", None),
            P(("slave", "master"), None),
            P(("slave", "master"), None, None),
        ),
        check_vma=False,
    )
```

```python
import functools

import jax
import jax.numpy as jnp
from jax import lax
from jax.experimental import pallas as pl
from jax.experimental.pallas import tpu as pltpu
from jax.sharding import PartitionSpec as P

GAUSS = 16
ITERS = 2
GROUP = 64


def tile_kernel(group, sidx_ref, nidx_ref, mreq_ref, slave_ref, basis_hbm, w_ref, out_ref, recv, sems):
    need = recv.shape[0]

    @pl.when(pl.program_id(0) == 0)
    def _():
        for r in range(need):
            pltpu.make_async_copy(basis_hbm.at[mreq_ref[r]], recv.at[r], sems.at[r]).start()
        for r in range(need):
            pltpu.make_async_copy(basis_hbm.at[0], recv.at[r], sems.at[r]).wait()

    base = pl.program_id(0) * group
    for g in range(group):
        s = sidx_ref[base + g]
        r = nidx_ref[base + g]
        left = slave_ref[s]
        w = w_ref[pl.ds(g, 1), :]
        right = (recv[r].astype(jnp.float32) * w).astype(jnp.bfloat16)
        tile = lax.dot_general(
            left, right, (((1,), (1,)), ((), ())), preferred_element_type=jnp.float32
        )
        out_ref[g] = tile.astype(out_ref.dtype)


def build_tiles(slave_basis, every_basis, request, pair_slave, pair_need, weights):
    pairs = weights.shape[0]
    nodes, qpts = slave_basis.shape[1], slave_basis.shape[2]
    need = request.shape[0]
    group = GROUP
    grid_spec = pltpu.PrefetchScalarGridSpec(
        num_scalar_prefetch=3,
        grid=(pairs // group,),
        in_specs=[
            pl.BlockSpec(slave_basis.shape, lambda i, s, n, m: (0, 0, 0)),
            pl.BlockSpec(memory_space=pl.ANY),
            pl.BlockSpec((group, qpts), lambda i, s, n, m: (i, 0)),
        ],
        out_specs=pl.BlockSpec((group, nodes, nodes), lambda i, s, n, m: (i, 0, 0)),
        scratch_shapes=[
            pltpu.VMEM((need, nodes, qpts), jnp.bfloat16),
            pltpu.SemaphoreType.DMA((need,)),
        ],
    )
    cost = pl.CostEstimate(
        flops=2 * pairs * nodes * nodes * qpts,
        bytes_accessed=pairs * nodes * nodes * 2 + need * nodes * qpts * 2 + pairs * qpts * 4,
        transcendentals=0,
    )
    return pl.pallas_call(
        functools.partial(tile_kernel, group),
        grid_spec=grid_spec,
        out_shape=jax.ShapeDtypeStruct((pairs, nodes, nodes), jnp.bfloat16),
        compiler_params=pltpu.CompilerParams(
            vmem_limit_bytes=48 * 1024 * 1024, dimension_semantics=("arbitrary",)
        ),
        cost_estimate=cost,
    )(pair_slave, pair_need, request, slave_basis, every_basis, weights)


def master_sum(x):
    count = lax.axis_size("master")
    spread = jnp.broadcast_to(x[None], (count,) + x.shape)
    got = lax.all_to_all(spread, "master", split_axis=0, concat_axis=0, tiled=True)
    return jnp.sum(got, axis=0)


def on_device(
    slave_basis,
    master_basis,
    slave_gap,
    master_disp,
    pressure,
    active,
    need_owner,
    need_slot,
    pair_need,
    pair_slave,
    pair_segs,
    pair_weight,
):
    high = lax.Precision.HIGHEST
    everyone = ("slave", "master")
    peers = lax.axis_size(everyone)
    mb_dev = master_basis.shape[0]
    need_dev = need_slot.shape[0]
    qpts = slave_basis.shape[2]
    owner = need_owner[:, 0]
    request = owner * mb_dev + need_slot
    every_basis = lax.all_gather(master_basis, everyone, axis=0, tiled=True)

    limit = GAUSS * pair_segs
    weights = jnp.where(
        jnp.arange(qpts, dtype=jnp.int32)[None, :] < limit[:, None],
        pair_weight,
        jnp.zeros_like(pair_weight),
    )
    slave_count = slave_basis.shape[0]
    slave_onehot = (
        pair_slave[None, :] == jnp.arange(slave_count, dtype=jnp.int32)[:, None]
    ).astype(jnp.float32)
    need_onehot = (pair_need[None, :] == jnp.arange(need_dev, dtype=jnp.int32)[:, None]).astype(
        jnp.float32
    )
    mblocks = peers * mb_dev
    block_onehot = (request[None, :] == jnp.arange(mblocks, dtype=jnp.int32)[:, None]).astype(
        jnp.float32
    )
    slave_weight = jnp.dot(slave_onehot, weights, precision=high)
    slave_float = slave_basis.astype(jnp.float32)
    master_float = master_basis.astype(jnp.float32)
    squares = jnp.square(slave_float)
    lump_part = jnp.einsum("snq,sq->sn", squares, slave_weight, precision=high)

    stored = build_tiles(slave_basis, every_basis, request, pair_slave, pair_need, weights)
    lam = pressure
    disp = master_disp
    flags = active == 1
    root_lump = None
    for update in range(ITERS):
        own_proj = jnp.einsum("mnq,mn->mq", master_float, disp, precision=high)
        outgoing_proj = jnp.broadcast_to(own_proj[None], (peers,) + own_proj.shape)
        returned = lax.all_to_all(outgoing_proj, everyone, split_axis=0, concat_axis=0, tiled=True)
        need_proj = returned.reshape(mblocks, qpts)[request]
        pair_terms = weights * need_proj[pair_need]
        slave_terms = jnp.dot(slave_onehot, pair_terms, precision=high)
        partial_coupled = jnp.einsum("snq,sq->sn", slave_float, slave_terms, precision=high)
        if update == 0:
            both = master_sum(jnp.stack([lump_part, partial_coupled]))
            root_lump = jnp.sqrt(1.0 + both[0])
            coupled = both[1]
        else:
            coupled = master_sum(partial_coupled)
        gap = slave_gap - coupled / root_lump
        lam = jnp.where(flags, lam - 1.0 * gap, jnp.zeros_like(lam))
        slave_proj = jnp.einsum("snq,sn->sq", slave_float, lam, precision=high)
        need_load = jnp.dot(need_onehot, weights * slave_proj[pair_slave], precision=high)
        outbound = jnp.dot(block_onehot, need_load, precision=high)
        inbound = lax.all_to_all(
            outbound.reshape(peers, mb_dev, qpts), everyone, split_axis=0, concat_axis=0, tiled=True
        )
        if update == ITERS - 1:
            stored, inbound = lax.optimization_barrier((stored, inbound))
        own_load = jnp.sum(inbound, axis=0)
        force = jnp.einsum("mnq,mq->mn", master_float, own_load, precision=high)
        disp = disp - 0.05 * force
    return (lam, disp, stored)


def solution(mesh):
    return jax.shard_map(
        on_device,
        mesh=mesh,
        in_specs=(
            P("slave", None, None),
            P(("slave", "master"), None, None),
            P("slave", None),
            P(("slave", "master"), None),
            P("slave", None),
            P("slave", None),
            P(("slave", "master"), None),
            P(("slave", "master")),
            P(("slave", "master")),
            P(("slave", "master")),
            P(("slave", "master")),
            P(("slave", "master"), None),
        ),
        out_specs=(
            P("slave", None),
            P(("slave", "master"), None),
            P(("slave", "master"), None, None),
        ),
        check_vma=False,
    )
```

```python
import functools

import jax
import jax.numpy as jnp
from jax import lax
from jax.experimental import pallas as pl
from jax.experimental.pallas import tpu as pltpu
from jax.sharding import PartitionSpec as P

GAUSS = 16
ITERS = 2
GROUP = 64


def tile_kernel(group, first, sidx_ref, nidx_ref, mreq_ref, slave_ref, basis_hbm, w_ref, *rest):
    out_ref, recv, sems = rest[-3:]
    need = recv.shape[0]

    @pl.when(pl.program_id(0) == 0)
    def _():
        for r in range(need):
            pltpu.make_async_copy(basis_hbm.at[mreq_ref[r]], recv.at[r], sems.at[r]).start()
        for r in range(need):
            pltpu.make_async_copy(basis_hbm.at[0], recv.at[r], sems.at[r]).wait()

    base = (pl.program_id(0) + first) * group
    for g in range(group):
        s = sidx_ref[base + g]
        r = nidx_ref[base + g]
        left = slave_ref[s]
        w = w_ref[pl.ds(g, 1), :]
        right = (recv[r].astype(jnp.float32) * w).astype(jnp.bfloat16)
        tile = lax.dot_general(
            left, right, (((1,), (1,)), ((), ())), preferred_element_type=jnp.float32
        )
        out_ref[g] = tile.astype(out_ref.dtype)


def build_tiles(slave_basis, every_basis, request, pair_slave, pair_need, weights, part, into=None):
    pairs = weights.shape[0]
    nodes, qpts = slave_basis.shape[1], slave_basis.shape[2]
    need = request.shape[0]
    group = GROUP
    steps = pairs // group // 2
    first = part * steps
    extra = [] if into is None else [pl.BlockSpec(memory_space=pl.ANY)]
    grid_spec = pltpu.PrefetchScalarGridSpec(
        num_scalar_prefetch=3,
        grid=(steps,),
        in_specs=[
            pl.BlockSpec(slave_basis.shape, lambda i, s, n, m: (0, 0, 0)),
            pl.BlockSpec(memory_space=pl.ANY),
            pl.BlockSpec((group, qpts), lambda i, s, n, m: (i + first, 0)),
        ]
        + extra,
        out_specs=pl.BlockSpec((group, nodes, nodes), lambda i, s, n, m: (i + first, 0, 0)),
        scratch_shapes=[
            pltpu.VMEM((need, nodes, qpts), jnp.bfloat16),
            pltpu.SemaphoreType.DMA((need,)),
        ],
    )
    cost = pl.CostEstimate(
        flops=pairs * nodes * nodes * qpts,
        bytes_accessed=pairs * nodes * nodes + need * nodes * qpts * 2 + pairs * qpts * 2,
        transcendentals=0,
    )
    operands = [pair_slave, pair_need, request, slave_basis, every_basis, weights]
    aliases = {}
    if into is not None:
        aliases = {len(operands): 0}
        operands.append(into)
    return pl.pallas_call(
        functools.partial(tile_kernel, group, first),
        grid_spec=grid_spec,
        out_shape=jax.ShapeDtypeStruct((pairs, nodes, nodes), jnp.bfloat16),
        compiler_params=pltpu.CompilerParams(
            vmem_limit_bytes=48 * 1024 * 1024, dimension_semantics=("arbitrary",)
        ),
        cost_estimate=cost,
        input_output_aliases=aliases,
    )(*operands)


def master_sum(x, tied=None):
    count = lax.axis_size("master")
    spread = jnp.broadcast_to(x[None], (count,) + x.shape)
    got = lax.all_to_all(spread, "master", split_axis=0, concat_axis=0, tiled=True)
    if tied is not None:
        tied, got = lax.optimization_barrier((tied, got))
    return jnp.sum(got, axis=0), tied


def on_device(
    slave_basis,
    master_basis,
    slave_gap,
    master_disp,
    pressure,
    active,
    need_owner,
    need_slot,
    pair_need,
    pair_slave,
    pair_segs,
    pair_weight,
):
    high = lax.Precision.HIGHEST
    everyone = ("slave", "master")
    peers = lax.axis_size(everyone)
    mb_dev = master_basis.shape[0]
    need_dev = need_slot.shape[0]
    qpts = slave_basis.shape[2]
    owner = need_owner[:, 0]
    request = owner * mb_dev + need_slot
    every_basis = lax.all_gather(master_basis, everyone, axis=0, tiled=True)

    limit = GAUSS * pair_segs
    weights = jnp.where(
        jnp.arange(qpts, dtype=jnp.int32)[None, :] < limit[:, None],
        pair_weight,
        jnp.zeros_like(pair_weight),
    )
    slave_count = slave_basis.shape[0]
    slave_onehot = (
        pair_slave[None, :] == jnp.arange(slave_count, dtype=jnp.int32)[:, None]
    ).astype(jnp.float32)
    need_onehot = (pair_need[None, :] == jnp.arange(need_dev, dtype=jnp.int32)[:, None]).astype(
        jnp.float32
    )
    mblocks = peers * mb_dev
    block_onehot = (request[None, :] == jnp.arange(mblocks, dtype=jnp.int32)[:, None]).astype(
        jnp.float32
    )
    slave_weight = jnp.dot(slave_onehot, weights, precision=high)
    slave_float = slave_basis.astype(jnp.float32)
    master_float = master_basis.astype(jnp.float32)
    squares = jnp.square(slave_float)
    lump_part = jnp.einsum("snq,sq->sn", squares, slave_weight, precision=high)

    tile_args = (slave_basis, every_basis, request, pair_slave, pair_need, weights)
    lam = pressure
    disp = master_disp
    flags = active == 1
    root_lump = None
    for update in range(ITERS):
        own_proj = jnp.einsum("mnq,mn->mq", master_float, disp, precision=high)
        outgoing_proj = jnp.broadcast_to(own_proj[None], (peers,) + own_proj.shape)
        returned = lax.all_to_all(outgoing_proj, everyone, split_axis=0, concat_axis=0, tiled=True)
        need_proj = returned.reshape(mblocks, qpts)[request]
        pair_terms = weights * need_proj[pair_need]
        slave_terms = jnp.dot(slave_onehot, pair_terms, precision=high)
        partial_coupled = jnp.einsum("snq,sq->sn", slave_float, slave_terms, precision=high)
        if update == 0:
            both, _ = master_sum(jnp.stack([lump_part, partial_coupled]))
            root_lump = jnp.sqrt(1.0 + both[0])
            coupled = both[1]
        else:
            coupled, stored = master_sum(partial_coupled, build_tiles(*tile_args, 0))
        gap = slave_gap - coupled / root_lump
        lam = jnp.where(flags, lam - 1.0 * gap, jnp.zeros_like(lam))
        slave_proj = jnp.einsum("snq,sn->sq", slave_float, lam, precision=high)
        need_load = jnp.dot(need_onehot, weights * slave_proj[pair_slave], precision=high)
        outbound = jnp.dot(block_onehot, need_load, precision=high)
        inbound = lax.all_to_all(
            outbound.reshape(peers, mb_dev, qpts), everyone, split_axis=0, concat_axis=0, tiled=True
        )
        if update == ITERS - 1:
            stored = build_tiles(*tile_args, 1, stored)
            stored, inbound = lax.optimization_barrier((stored, inbound))
        own_load = jnp.sum(inbound, axis=0)
        force = jnp.einsum("mnq,mq->mn", master_float, own_load, precision=high)
        disp = disp - 0.05 * force
    return (lam, disp, stored)


def solution(mesh):
    return jax.shard_map(
        on_device,
        mesh=mesh,
        in_specs=(
            P("slave", None, None),
            P(("slave", "master"), None, None),
            P("slave", None),
            P(("slave", "master"), None),
            P("slave", None),
            P("slave", None),
            P(("slave", "master"), None),
            P(("slave", "master")),
            P(("slave", "master")),
            P(("slave", "master")),
            P(("slave", "master")),
            P(("slave", "master"), None),
        ),
        out_specs=(
            P("slave", None),
            P(("slave", "master"), None),
            P(("slave", "master"), None, None),
        ),
        check_vma=False,
    )
```

```python
import functools

import jax
import jax.numpy as jnp
from jax import lax
from jax.experimental import pallas as pl
from jax.experimental.pallas import tpu as pltpu
from jax.sharding import PartitionSpec as P

GAUSS = 16
ITERS = 2
GROUP = 64


def tile_kernel(group, sidx_ref, nidx_ref, mreq_ref, slave_ref, basis_hbm, w_ref, out_ref, recv, sems):
    need = recv.shape[0]

    @pl.when(pl.program_id(0) == 0)
    def _():
        for r in range(need):
            pltpu.make_async_copy(basis_hbm.at[mreq_ref[r]], recv.at[r], sems.at[r]).start()
        for r in range(need):
            pltpu.make_async_copy(basis_hbm.at[0], recv.at[r], sems.at[r]).wait()

    base = pl.program_id(0) * group
    for g in range(group):
        s = sidx_ref[base + g]
        r = nidx_ref[base + g]
        left = slave_ref[s]
        w = w_ref[pl.ds(g, 1), :]
        right = (recv[r].astype(jnp.float32) * w).astype(jnp.bfloat16)
        tile = lax.dot_general(
            left, right, (((1,), (1,)), ((), ())), preferred_element_type=jnp.float32
        )
        out_ref[g] = tile.astype(out_ref.dtype)


def build_tiles(slave_basis, every_basis, request, pair_slave, pair_need, weights):
    pairs = weights.shape[0]
    nodes, qpts = slave_basis.shape[1], slave_basis.shape[2]
    need = request.shape[0]
    group = GROUP
    grid_spec = pltpu.PrefetchScalarGridSpec(
        num_scalar_prefetch=3,
        grid=(pairs // group,),
        in_specs=[
            pl.BlockSpec(slave_basis.shape, lambda i, s, n, m: (0, 0, 0)),
            pl.BlockSpec(memory_space=pl.ANY),
            pl.BlockSpec((group, qpts), lambda i, s, n, m: (i, 0)),
        ],
        out_specs=pl.BlockSpec((group, nodes, nodes), lambda i, s, n, m: (i, 0, 0)),
        scratch_shapes=[
            pltpu.VMEM((need, nodes, qpts), jnp.bfloat16),
            pltpu.SemaphoreType.DMA((need,)),
        ],
    )
    cost = pl.CostEstimate(
        flops=2 * pairs * nodes * nodes * qpts,
        bytes_accessed=pairs * nodes * nodes * 2 + need * nodes * qpts * 2 + pairs * qpts * 4,
        transcendentals=0,
    )
    return pl.pallas_call(
        functools.partial(tile_kernel, group),
        grid_spec=grid_spec,
        out_shape=jax.ShapeDtypeStruct((pairs, nodes, nodes), jnp.bfloat16),
        compiler_params=pltpu.CompilerParams(
            vmem_limit_bytes=48 * 1024 * 1024, dimension_semantics=("arbitrary",)
        ),
        cost_estimate=cost,
    )(pair_slave, pair_need, request, slave_basis, every_basis, weights)


def master_sum(x):
    count = lax.axis_size("master")
    spread = jnp.broadcast_to(x[None], (count,) + x.shape)
    got = lax.all_to_all(spread, "master", split_axis=0, concat_axis=0, tiled=True)
    return jnp.sum(got, axis=0)


def on_device(
    slave_basis,
    master_basis,
    slave_gap,
    master_disp,
    pressure,
    active,
    need_owner,
    need_slot,
    pair_need,
    pair_slave,
    pair_segs,
    pair_weight,
):
    high = lax.Precision.HIGHEST
    everyone = ("slave", "master")
    peers = lax.axis_size(everyone)
    mb_dev = master_basis.shape[0]
    need_dev = need_slot.shape[0]
    qpts = slave_basis.shape[2]
    owner = need_owner[:, 0]
    request = owner * mb_dev + need_slot
    every_basis = lax.all_gather(master_basis, everyone, axis=0, tiled=True)

    limit = GAUSS * pair_segs
    weights = jnp.where(
        jnp.arange(qpts, dtype=jnp.int32)[None, :] < limit[:, None],
        pair_weight,
        jnp.zeros_like(pair_weight),
    )
    slave_count = slave_basis.shape[0]
    slave_onehot = (
        pair_slave[None, :] == jnp.arange(slave_count, dtype=jnp.int32)[:, None]
    ).astype(jnp.float32)
    need_onehot = (pair_need[None, :] == jnp.arange(need_dev, dtype=jnp.int32)[:, None]).astype(
        jnp.float32
    )
    mblocks = peers * mb_dev
    block_onehot = (request[None, :] == jnp.arange(mblocks, dtype=jnp.int32)[:, None]).astype(
        jnp.float32
    )
    slave_weight = jnp.dot(slave_onehot, weights, precision=high)
    slave_float = slave_basis.astype(jnp.float32)
    master_float = master_basis.astype(jnp.float32)
    squares = jnp.square(slave_float)
    lump_part = jnp.sum(squares * slave_weight[:, None, :], axis=2)

    stored = build_tiles(slave_basis, every_basis, request, pair_slave, pair_need, weights)
    lam = pressure
    disp = master_disp
    flags = active == 1
    root_lump = None
    for update in range(ITERS):
        own_proj = jnp.sum(master_float * disp[:, :, None], axis=1)
        outgoing_proj = jnp.broadcast_to(own_proj[None], (peers,) + own_proj.shape)
        returned = lax.all_to_all(outgoing_proj, everyone, split_axis=0, concat_axis=0, tiled=True)
        need_proj = returned.reshape(mblocks, qpts)[request]
        pair_terms = weights * need_proj[pair_need]
        slave_terms = jnp.dot(slave_onehot, pair_terms, precision=high)
        partial_coupled = jnp.sum(slave_float * slave_terms[:, None, :], axis=2)
        if update == 0:
            both = master_sum(jnp.stack([lump_part, partial_coupled]))
            root_lump = jnp.sqrt(1.0 + both[0])
            coupled = both[1]
        else:
            coupled = master_sum(partial_coupled)
        gap = slave_gap - coupled / root_lump
        lam = jnp.where(flags, lam - 1.0 * gap, jnp.zeros_like(lam))
        slave_proj = jnp.sum(slave_float * lam[:, :, None], axis=1)
        need_load = jnp.dot(need_onehot, weights * slave_proj[pair_slave], precision=high)
        outbound = jnp.dot(block_onehot, need_load, precision=high)
        inbound = lax.all_to_all(
            outbound.reshape(peers, mb_dev, qpts), everyone, split_axis=0, concat_axis=0, tiled=True
        )
        if update == ITERS - 1:
            stored, inbound = lax.optimization_barrier((stored, inbound))
        own_load = jnp.sum(inbound, axis=0)
        force = jnp.sum(master_float * own_load[:, None, :], axis=2)
        disp = disp - 0.05 * force
    return (lam, disp, stored)


def solution(mesh):
    return jax.shard_map(
        on_device,
        mesh=mesh,
        in_specs=(
            P("slave", None, None),
            P(("slave", "master"), None, None),
            P("slave", None),
            P(("slave", "master"), None),
            P("slave", None),
            P("slave", None),
            P(("slave", "master"), None),
            P(("slave", "master")),
            P(("slave", "master")),
            P(("slave", "master")),
            P(("slave", "master")),
            P(("slave", "master"), None),
        ),
        out_specs=(
            P("slave", None),
            P(("slave", "master"), None),
            P(("slave", "master"), None, None),
        ),
        check_vma=False,
    )
```

```python
import functools

import jax
import jax.numpy as jnp
from jax import lax
from jax.experimental import pallas as pl
from jax.experimental.pallas import tpu as pltpu
from jax.sharding import PartitionSpec as P

GAUSS = 16
ITERS = 2
GROUP = 64


def tile_kernel(group, sidx_ref, nidx_ref, mreq_ref, slave_ref, basis_hbm, w_ref, out_ref, recv, sems):
    need = recv.shape[0]

    @pl.when(pl.program_id(0) == 0)
    def _():
        for r in range(need):
            pltpu.make_async_copy(basis_hbm.at[mreq_ref[r]], recv.at[r], sems.at[r]).start()
        for r in range(need):
            pltpu.make_async_copy(basis_hbm.at[0], recv.at[r], sems.at[r]).wait()

    base = pl.program_id(0) * group
    for g in range(group):
        s = sidx_ref[base + g]
        r = nidx_ref[base + g]
        left = slave_ref[s]
        w = w_ref[pl.ds(g, 1), :]
        right = (recv[r].astype(jnp.float32) * w).astype(jnp.bfloat16)
        tile = lax.dot_general(
            left, right, (((1,), (1,)), ((), ())), preferred_element_type=jnp.float32
        )
        out_ref[g] = tile.astype(out_ref.dtype)


def build_tiles(slave_basis, every_basis, request, pair_slave, pair_need, weights):
    pairs = weights.shape[0]
    nodes, qpts = slave_basis.shape[1], slave_basis.shape[2]
    need = request.shape[0]
    group = GROUP
    grid_spec = pltpu.PrefetchScalarGridSpec(
        num_scalar_prefetch=3,
        grid=(pairs // group,),
        in_specs=[
            pl.BlockSpec(slave_basis.shape, lambda i, s, n, m: (0, 0, 0)),
            pl.BlockSpec(memory_space=pl.ANY),
            pl.BlockSpec((group, qpts), lambda i, s, n, m: (i, 0)),
        ],
        out_specs=pl.BlockSpec((group, nodes, nodes), lambda i, s, n, m: (i, 0, 0)),
        scratch_shapes=[
            pltpu.VMEM((need, nodes, qpts), jnp.bfloat16),
            pltpu.SemaphoreType.DMA((need,)),
        ],
    )
    cost = pl.CostEstimate(
        flops=2 * pairs * nodes * nodes * qpts,
        bytes_accessed=pairs * nodes * nodes * 2 + need * nodes * qpts * 2 + pairs * qpts * 4,
        transcendentals=0,
    )
    return pl.pallas_call(
        functools.partial(tile_kernel, group),
        grid_spec=grid_spec,
        out_shape=jax.ShapeDtypeStruct((pairs, nodes, nodes), jnp.bfloat16),
        compiler_params=pltpu.CompilerParams(
            vmem_limit_bytes=48 * 1024 * 1024, dimension_semantics=("arbitrary",)
        ),
        cost_estimate=cost,
    )(pair_slave, pair_need, request, slave_basis, every_basis, weights)


def master_sum(x):
    count = lax.axis_size("master")
    spread = jnp.broadcast_to(x[None], (count,) + x.shape)
    got = lax.all_to_all(spread, "master", split_axis=0, concat_axis=0, tiled=True)
    return jnp.sum(got, axis=0)


def on_device(
    slave_basis,
    master_basis,
    slave_gap,
    master_disp,
    pressure,
    active,
    need_owner,
    need_slot,
    pair_need,
    pair_slave,
    pair_segs,
    pair_weight,
):
    high = lax.Precision.HIGHEST
    everyone = ("slave", "master")
    peers = lax.axis_size(everyone)
    mb_dev = master_basis.shape[0]
    qpts = slave_basis.shape[2]
    owner = need_owner[:, 0]
    request = owner * mb_dev + need_slot
    every_basis = lax.all_gather(master_basis, everyone, axis=0, tiled=True)

    limit = GAUSS * pair_segs
    weights = jnp.where(
        jnp.arange(qpts, dtype=jnp.int32)[None, :] < limit[:, None],
        pair_weight,
        jnp.zeros_like(pair_weight),
    )
    slave_count = slave_basis.shape[0]
    slave_onehot = (
        pair_slave[None, :] == jnp.arange(slave_count, dtype=jnp.int32)[:, None]
    ).astype(jnp.float32)
    mblocks = peers * mb_dev
    pair_block = request[pair_need]
    block_onehot = (
        pair_block[None, :] == jnp.arange(mblocks, dtype=jnp.int32)[:, None]
    ).astype(jnp.float32)
    slave_weight = jnp.dot(slave_onehot, weights, precision=high)
    slave_float = slave_basis.astype(jnp.float32)
    master_float = master_basis.astype(jnp.float32)
    squares = jnp.square(slave_float)
    lump_part = jnp.sum(squares * slave_weight[:, None, :], axis=2)

    stored = build_tiles(slave_basis, every_basis, request, pair_slave, pair_need, weights)
    lam = pressure
    disp = master_disp
    flags = active == 1
    root_lump = None
    for update in range(ITERS):
        own_proj = jnp.sum(master_float * disp[:, :, None], axis=1)
        outgoing_proj = jnp.broadcast_to(own_proj[None], (peers,) + own_proj.shape)
        returned = lax.all_to_all(outgoing_proj, everyone, split_axis=0, concat_axis=0, tiled=True)
        pair_terms = weights * returned.reshape(mblocks, qpts)[pair_block]
        slave_terms = jnp.dot(slave_onehot, pair_terms, precision=high)
        partial_coupled = jnp.sum(slave_float * slave_terms[:, None, :], axis=2)
        if update == 0:
            both = master_sum(jnp.stack([lump_part, partial_coupled]))
            root_lump = jnp.sqrt(1.0 + both[0])
            coupled = both[1]
        else:
            coupled = master_sum(partial_coupled)
        gap = slave_gap - coupled / root_lump
        lam = jnp.where(flags, lam - 1.0 * gap, jnp.zeros_like(lam))
        slave_proj = jnp.sum(slave_float * lam[:, :, None], axis=1)
        outbound = jnp.dot(block_onehot, weights * slave_proj[pair_slave], precision=high)
        inbound = lax.all_to_all(
            outbound.reshape(peers, mb_dev, qpts), everyone, split_axis=0, concat_axis=0, tiled=True
        )
        if update == ITERS - 1:
            stored, inbound = lax.optimization_barrier((stored, inbound))
        own_load = jnp.sum(inbound, axis=0)
        force = jnp.sum(master_float * own_load[:, None, :], axis=2)
        disp = disp - 0.05 * force
    return (lam, disp, stored)


def solution(mesh):
    return jax.shard_map(
        on_device,
        mesh=mesh,
        in_specs=(
            P("slave", None, None),
            P(("slave", "master"), None, None),
            P("slave", None),
            P(("slave", "master"), None),
            P("slave", None),
            P("slave", None),
            P(("slave", "master"), None),
            P(("slave", "master")),
            P(("slave", "master")),
            P(("slave", "master")),
            P(("slave", "master")),
            P(("slave", "master"), None),
        ),
        out_specs=(
            P("slave", None),
            P(("slave", "master"), None),
            P(("slave", "master"), None, None),
        ),
        check_vma=False,
    )
```

```python
import functools

import jax
import jax.numpy as jnp
from jax import lax
from jax.experimental import pallas as pl
from jax.experimental.pallas import tpu as pltpu
from jax.sharding import PartitionSpec as P

GAUSS = 16
ITERS = 2
GROUP = 64


def tile_kernel(group, sidx_ref, nidx_ref, mreq_ref, slave_ref, basis_hbm, w_ref, out_ref, recv, sems):
    need = recv.shape[0]

    @pl.when(pl.program_id(0) == 0)
    def _():
        for r in range(need):
            pltpu.make_async_copy(basis_hbm.at[mreq_ref[r]], recv.at[r], sems.at[r]).start()
        for r in range(need):
            pltpu.make_async_copy(basis_hbm.at[0], recv.at[r], sems.at[r]).wait()

    base = pl.program_id(0) * group
    for g in range(group):
        s = sidx_ref[base + g]
        r = nidx_ref[base + g]
        left = slave_ref[s]
        w = w_ref[pl.ds(g, 1), :]
        right = (recv[r].astype(jnp.float32) * w).astype(jnp.bfloat16)
        tile = lax.dot_general(
            left, right, (((1,), (1,)), ((), ())), preferred_element_type=jnp.float32
        )
        out_ref[g] = tile.astype(out_ref.dtype)


def build_tiles(slave_basis, every_basis, request, pair_slave, pair_need, weights):
    pairs = weights.shape[0]
    nodes, qpts = slave_basis.shape[1], slave_basis.shape[2]
    need = request.shape[0]
    group = GROUP
    grid_spec = pltpu.PrefetchScalarGridSpec(
        num_scalar_prefetch=3,
        grid=(pairs // group,),
        in_specs=[
            pl.BlockSpec(slave_basis.shape, lambda i, s, n, m: (0, 0, 0)),
            pl.BlockSpec(memory_space=pl.ANY),
            pl.BlockSpec((group, qpts), lambda i, s, n, m: (i, 0)),
        ],
        out_specs=pl.BlockSpec((group, nodes, nodes), lambda i, s, n, m: (i, 0, 0)),
        scratch_shapes=[
            pltpu.VMEM((need, nodes, qpts), jnp.bfloat16),
            pltpu.SemaphoreType.DMA((need,)),
        ],
    )
    cost = pl.CostEstimate(
        flops=2 * pairs * nodes * nodes * qpts,
        bytes_accessed=pairs * nodes * nodes * 2 + need * nodes * qpts * 2 + pairs * qpts * 4,
        transcendentals=0,
    )
    return pl.pallas_call(
        functools.partial(tile_kernel, group),
        grid_spec=grid_spec,
        out_shape=jax.ShapeDtypeStruct((pairs, nodes, nodes), jnp.bfloat16),
        compiler_params=pltpu.CompilerParams(
            vmem_limit_bytes=48 * 1024 * 1024, dimension_semantics=("arbitrary",)
        ),
        cost_estimate=cost,
    )(pair_slave, pair_need, request, slave_basis, every_basis, weights)


def on_device(
    slave_basis,
    master_basis,
    slave_gap,
    master_disp,
    pressure,
    active,
    need_owner,
    need_slot,
    pair_need,
    pair_slave,
    pair_segs,
    pair_weight,
):
    high = lax.Precision.HIGHEST
    everyone = ("slave", "master")
    peers = lax.axis_size(everyone)
    mb_dev = master_basis.shape[0]
    qpts = slave_basis.shape[2]
    owner = need_owner[:, 0]
    request = owner * mb_dev + need_slot
    every_basis = lax.all_gather(master_basis, everyone, axis=0, tiled=True)

    limit = GAUSS * pair_segs
    weights = jnp.where(
        jnp.arange(qpts, dtype=jnp.int32)[None, :] < limit[:, None],
        pair_weight,
        jnp.zeros_like(pair_weight),
    )
    slave_count = slave_basis.shape[0]
    slave_onehot = (
        pair_slave[None, :] == jnp.arange(slave_count, dtype=jnp.int32)[:, None]
    ).astype(jnp.float32)
    mblocks = peers * mb_dev
    pair_block = request[pair_need]
    block_onehot = (
        pair_block[None, :] == jnp.arange(mblocks, dtype=jnp.int32)[:, None]
    ).astype(jnp.float32)
    group = lax.axis_size("master")
    weights_group = lax.all_to_all(
        jnp.broadcast_to(weights[None], (group,) + weights.shape), "master", 0, 0, tiled=True
    ).reshape(-1, qpts)
    index_group = lax.all_to_all(
        jnp.broadcast_to(jnp.stack([pair_block, pair_slave])[None], (group, 2) + pair_block.shape),
        "master",
        0,
        0,
        tiled=True,
    )
    block_group = index_group[:, 0].reshape(-1)
    slave_group = index_group[:, 1].reshape(-1)
    group_onehot = (
        slave_group[None, :] == jnp.arange(slave_count, dtype=jnp.int32)[:, None]
    ).astype(jnp.float32)
    slave_weight = jnp.dot(group_onehot, weights_group, precision=high)
    slave_float = slave_basis.astype(jnp.float32)
    master_float = master_basis.astype(jnp.float32)
    squares = jnp.square(slave_float)
    lump_part = jnp.sum(squares * slave_weight[:, None, :], axis=2)

    stored = build_tiles(slave_basis, every_basis, request, pair_slave, pair_need, weights)
    lam = pressure
    disp = master_disp
    flags = active == 1
    root_lump = None
    for update in range(ITERS):
        own_proj = jnp.sum(master_float * disp[:, :, None], axis=1)
        outgoing_proj = jnp.broadcast_to(own_proj[None], (peers,) + own_proj.shape)
        returned = lax.all_to_all(outgoing_proj, everyone, split_axis=0, concat_axis=0, tiled=True)
        pair_terms = weights_group * returned.reshape(mblocks, qpts)[block_group]
        slave_terms = jnp.dot(group_onehot, pair_terms, precision=high)
        partial_coupled = jnp.sum(slave_float * slave_terms[:, None, :], axis=2)
        if update == 0:
            root_lump = jnp.sqrt(1.0 + lump_part)
        coupled = partial_coupled
        gap = slave_gap - coupled / root_lump
        lam = jnp.where(flags, lam - 1.0 * gap, jnp.zeros_like(lam))
        slave_proj = jnp.sum(slave_float * lam[:, :, None], axis=1)
        outbound = jnp.dot(block_onehot, weights * slave_proj[pair_slave], precision=high)
        inbound = lax.all_to_all(
            outbound.reshape(peers, mb_dev, qpts), everyone, split_axis=0, concat_axis=0, tiled=True
        )
        if update == ITERS - 1:
            stored, inbound = lax.optimization_barrier((stored, inbound))
        own_load = jnp.sum(inbound, axis=0)
        force = jnp.sum(master_float * own_load[:, None, :], axis=2)
        disp = disp - 0.05 * force
    return (lam, disp, stored)


def solution(mesh):
    return jax.shard_map(
        on_device,
        mesh=mesh,
        in_specs=(
            P("slave", None, None),
            P(("slave", "master"), None, None),
            P("slave", None),
            P(("slave", "master"), None),
            P("slave", None),
            P("slave", None),
            P(("slave", "master"), None),
            P(("slave", "master")),
            P(("slave", "master")),
            P(("slave", "master")),
            P(("slave", "master")),
            P(("slave", "master"), None),
        ),
        out_specs=(
            P("slave", None),
            P(("slave", "master"), None),
            P(("slave", "master"), None, None),
        ),
        check_vma=False,
    )
```

```python
import functools

import jax
import jax.numpy as jnp
from jax import lax
from jax.experimental import pallas as pl
from jax.experimental.pallas import tpu as pltpu
from jax.sharding import PartitionSpec as P

GAUSS = 16
ITERS = 2
GROUP = 64


def tile_kernel(
    group, sidx_ref, nidx_ref, mreq_ref, slave_ref, basis_hbm, w_ref, out_ref, recv, sems, landed
):
    need = recv.shape[0]

    @pl.when(pl.program_id(0) == 0)
    def _():
        for r in range(need):
            landed[r] = 0
            pltpu.make_async_copy(basis_hbm.at[mreq_ref[r]], recv.at[r], sems.at[r]).start()

    base = pl.program_id(0) * group
    for g in range(group):
        s = sidx_ref[base + g]
        r = nidx_ref[base + g]

        @pl.when(landed[r] == 0)
        def _():
            pltpu.make_async_copy(basis_hbm.at[0], recv.at[r], sems.at[r]).wait()
            landed[r] = 1

        left = slave_ref[s]
        w = w_ref[pl.ds(g, 1), :]
        right = (recv[r].astype(jnp.float32) * w).astype(jnp.bfloat16)
        tile = lax.dot_general(
            left, right, (((1,), (1,)), ((), ())), preferred_element_type=jnp.float32
        )
        out_ref[g] = tile.astype(out_ref.dtype)

    @pl.when(pl.program_id(0) == pl.num_programs(0) - 1)
    def _():
        for r in range(need):

            @pl.when(landed[r] == 0)
            def _():
                pltpu.make_async_copy(basis_hbm.at[0], recv.at[r], sems.at[r]).wait()


def build_tiles(slave_basis, every_basis, request, pair_slave, pair_need, weights):
    pairs = weights.shape[0]
    nodes, qpts = slave_basis.shape[1], slave_basis.shape[2]
    need = request.shape[0]
    group = GROUP
    grid_spec = pltpu.PrefetchScalarGridSpec(
        num_scalar_prefetch=3,
        grid=(pairs // group,),
        in_specs=[
            pl.BlockSpec(slave_basis.shape, lambda i, s, n, m: (0, 0, 0)),
            pl.BlockSpec(memory_space=pl.ANY),
            pl.BlockSpec((group, qpts), lambda i, s, n, m: (i, 0)),
        ],
        out_specs=pl.BlockSpec((group, nodes, nodes), lambda i, s, n, m: (i, 0, 0)),
        scratch_shapes=[
            pltpu.VMEM((need, nodes, qpts), jnp.bfloat16),
            pltpu.SemaphoreType.DMA((need,)),
            pltpu.SMEM((need,), jnp.int32),
        ],
    )
    cost = pl.CostEstimate(
        flops=2 * pairs * nodes * nodes * qpts,
        bytes_accessed=pairs * nodes * nodes * 2 + need * nodes * qpts * 2 + pairs * qpts * 4,
        transcendentals=0,
    )
    return pl.pallas_call(
        functools.partial(tile_kernel, group),
        grid_spec=grid_spec,
        out_shape=jax.ShapeDtypeStruct((pairs, nodes, nodes), jnp.bfloat16),
        compiler_params=pltpu.CompilerParams(
            vmem_limit_bytes=48 * 1024 * 1024, dimension_semantics=("arbitrary",)
        ),
        cost_estimate=cost,
    )(pair_slave, pair_need, request, slave_basis, every_basis, weights)


def master_sum(x):
    count = lax.axis_size("master")
    spread = jnp.broadcast_to(x[None], (count,) + x.shape)
    got = lax.all_to_all(spread, "master", split_axis=0, concat_axis=0, tiled=True)
    return jnp.sum(got, axis=0)


def on_device(
    slave_basis,
    master_basis,
    slave_gap,
    master_disp,
    pressure,
    active,
    need_owner,
    need_slot,
    pair_need,
    pair_slave,
    pair_segs,
    pair_weight,
):
    high = lax.Precision.HIGHEST
    everyone = ("slave", "master")
    peers = lax.axis_size(everyone)
    mb_dev = master_basis.shape[0]
    qpts = slave_basis.shape[2]
    owner = need_owner[:, 0]
    request = owner * mb_dev + need_slot
    every_basis = lax.all_gather(master_basis, everyone, axis=0, tiled=True)

    limit = GAUSS * pair_segs
    weights = jnp.where(
        jnp.arange(qpts, dtype=jnp.int32)[None, :] < limit[:, None],
        pair_weight,
        jnp.zeros_like(pair_weight),
    )
    slave_count = slave_basis.shape[0]
    slave_onehot = (
        pair_slave[None, :] == jnp.arange(slave_count, dtype=jnp.int32)[:, None]
    ).astype(jnp.float32)
    mblocks = peers * mb_dev
    pair_block = request[pair_need]
    block_onehot = (
        pair_block[None, :] == jnp.arange(mblocks, dtype=jnp.int32)[:, None]
    ).astype(jnp.float32)
    slave_weight = jnp.dot(slave_onehot, weights, precision=high)
    slave_float = slave_basis.astype(jnp.float32)
    master_float = master_basis.astype(jnp.float32)
    squares = jnp.square(slave_float)
    lump_part = jnp.sum(squares * slave_weight[:, None, :], axis=2)

    stored = build_tiles(slave_basis, every_basis, request, pair_slave, pair_need, weights)
    lam = pressure
    disp = master_disp
    flags = active == 1
    root_lump = None
    for update in range(ITERS):
        own_proj = jnp.sum(master_float * disp[:, :, None], axis=1)
        outgoing_proj = jnp.broadcast_to(own_proj[None], (peers,) + own_proj.shape)
        returned = lax.all_to_all(outgoing_proj, everyone, split_axis=0, concat_axis=0, tiled=True)
        pair_terms = weights * returned.reshape(mblocks, qpts)[pair_block]
        slave_terms = jnp.dot(slave_onehot, pair_terms, precision=high)
        partial_coupled = jnp.sum(slave_float * slave_terms[:, None, :], axis=2)
        if update == 0:
            both = master_sum(jnp.stack([lump_part, partial_coupled]))
            root_lump = jnp.sqrt(1.0 + both[0])
            coupled = both[1]
        else:
            coupled = master_sum(partial_coupled)
        gap = slave_gap - coupled / root_lump
        lam = jnp.where(flags, lam - 1.0 * gap, jnp.zeros_like(lam))
        slave_proj = jnp.sum(slave_float * lam[:, :, None], axis=1)
        outbound = jnp.dot(block_onehot, weights * slave_proj[pair_slave], precision=high)
        inbound = lax.all_to_all(
            outbound.reshape(peers, mb_dev, qpts), everyone, split_axis=0, concat_axis=0, tiled=True
        )
        if update == ITERS - 1:
            stored, inbound = lax.optimization_barrier((stored, inbound))
        own_load = jnp.sum(inbound, axis=0)
        force = jnp.sum(master_float * own_load[:, None, :], axis=2)
        disp = disp - 0.05 * force
    return (lam, disp, stored)


def solution(mesh):
    return jax.shard_map(
        on_device,
        mesh=mesh,
        in_specs=(
            P("slave", None, None),
            P(("slave", "master"), None, None),
            P("slave", None),
            P(("slave", "master"), None),
            P("slave", None),
            P("slave", None),
            P(("slave", "master"), None),
            P(("slave", "master")),
            P(("slave", "master")),
            P(("slave", "master")),
            P(("slave", "master")),
            P(("slave", "master"), None),
        ),
        out_specs=(
            P("slave", None),
            P(("slave", "master"), None),
            P(("slave", "master"), None, None),
        ),
        check_vma=False,
    )
```

```python
import functools

import jax
import jax.numpy as jnp
from jax import lax
from jax.experimental import pallas as pl
from jax.experimental.pallas import tpu as pltpu
from jax.sharding import PartitionSpec as P

GAUSS = 16
ITERS = 2
GROUP = 64


def tile_kernel(group, sidx_ref, nidx_ref, mreq_ref, slave_ref, basis_hbm, w_ref, out_ref, recv, sems):
    need = recv.shape[0]

    @pl.when(pl.program_id(0) == 0)
    def _():
        for r in range(need):
            pltpu.make_async_copy(basis_hbm.at[mreq_ref[r]], recv.at[r], sems.at[r]).start()
        for r in range(need):
            pltpu.make_async_copy(basis_hbm.at[0], recv.at[r], sems.at[r]).wait()

    base = pl.program_id(0) * group
    for g in range(group):
        s = sidx_ref[base + g]
        r = nidx_ref[base + g]
        left = slave_ref[s]
        w = w_ref[pl.ds(g, 1), :]
        right = (recv[r].astype(jnp.float32) * w).astype(jnp.bfloat16)
        tile = lax.dot_general(
            left, right, (((1,), (1,)), ((), ())), preferred_element_type=jnp.float32
        )
        out_ref[g] = tile.astype(out_ref.dtype)


def build_tiles(slave_basis, every_basis, request, pair_slave, pair_need, weights):
    pairs = weights.shape[0]
    nodes, qpts = slave_basis.shape[1], slave_basis.shape[2]
    need = request.shape[0]
    group = GROUP
    grid_spec = pltpu.PrefetchScalarGridSpec(
        num_scalar_prefetch=3,
        grid=(pairs // group,),
        in_specs=[
            pl.BlockSpec(slave_basis.shape, lambda i, s, n, m: (0, 0, 0)),
            pl.BlockSpec(memory_space=pl.ANY),
            pl.BlockSpec((group, qpts), lambda i, s, n, m: (i, 0)),
        ],
        out_specs=pl.BlockSpec((group, nodes, nodes), lambda i, s, n, m: (i, 0, 0)),
        scratch_shapes=[
            pltpu.VMEM((need, nodes, qpts), jnp.bfloat16),
            pltpu.SemaphoreType.DMA((need,)),
        ],
    )
    cost = pl.CostEstimate(
        flops=2 * pairs * nodes * nodes * qpts,
        bytes_accessed=pairs * nodes * nodes * 2 + need * nodes * qpts * 2 + pairs * qpts * 4,
        transcendentals=0,
    )
    return pl.pallas_call(
        functools.partial(tile_kernel, group),
        grid_spec=grid_spec,
        out_shape=jax.ShapeDtypeStruct((pairs, nodes, nodes), jnp.bfloat16),
        compiler_params=pltpu.CompilerParams(
            vmem_limit_bytes=48 * 1024 * 1024, dimension_semantics=("arbitrary",)
        ),
        cost_estimate=cost,
    )(pair_slave, pair_need, request, slave_basis, every_basis, weights)


def master_sum(x):
    count = lax.axis_size("master")
    spread = jnp.broadcast_to(x[None], (count,) + x.shape)
    got = lax.all_to_all(spread, "master", split_axis=0, concat_axis=0, tiled=True)
    return jnp.sum(got, axis=0)


def on_device(
    slave_basis,
    master_basis,
    slave_gap,
    master_disp,
    pressure,
    active,
    need_owner,
    need_slot,
    pair_need,
    pair_slave,
    pair_segs,
    pair_weight,
):
    high = lax.Precision.HIGHEST
    everyone = ("slave", "master")
    peers = lax.axis_size(everyone)
    mb_dev = master_basis.shape[0]
    qpts = slave_basis.shape[2]
    owner = need_owner[:, 0]
    request = owner * mb_dev + need_slot
    every_basis = lax.all_gather(master_basis, everyone, axis=0, tiled=True)

    limit = GAUSS * pair_segs
    weights = jnp.where(
        jnp.arange(qpts, dtype=jnp.int32)[None, :] < limit[:, None],
        pair_weight,
        jnp.zeros_like(pair_weight),
    )
    slave_count = slave_basis.shape[0]
    slave_onehot = (
        pair_slave[None, :] == jnp.arange(slave_count, dtype=jnp.int32)[:, None]
    ).astype(jnp.float32)
    mblocks = peers * mb_dev
    pair_block = request[pair_need]
    block_onehot = (
        pair_block[None, :] == jnp.arange(mblocks, dtype=jnp.int32)[:, None]
    ).astype(jnp.float32)
    slave_weight = jnp.dot(slave_onehot, weights, precision=high)
    slave_float = slave_basis.astype(jnp.float32)
    master_float = master_basis.astype(jnp.float32)
    squares = jnp.square(slave_float)
    lump_part = jnp.sum(squares * slave_weight[:, None, :], axis=2)
    gram = jnp.einsum("mnq,mnr->mqr", master_float, master_float, precision=high)

    stored = build_tiles(slave_basis, every_basis, request, pair_slave, pair_need, weights)
    lam = pressure
    disp = master_disp
    flags = active == 1
    root_lump = None
    own_proj = jnp.sum(master_float * disp[:, :, None], axis=1)
    for update in range(ITERS):
        outgoing_proj = jnp.broadcast_to(own_proj[None], (peers,) + own_proj.shape)
        returned = lax.all_to_all(outgoing_proj, everyone, split_axis=0, concat_axis=0, tiled=True)
        pair_terms = weights * returned.reshape(mblocks, qpts)[pair_block]
        slave_terms = jnp.dot(slave_onehot, pair_terms, precision=high)
        partial_coupled = jnp.sum(slave_float * slave_terms[:, None, :], axis=2)
        if update == 0:
            both = master_sum(jnp.stack([lump_part, partial_coupled]))
            root_lump = jnp.sqrt(1.0 + both[0])
            coupled = both[1]
        else:
            coupled = master_sum(partial_coupled)
        gap = slave_gap - coupled / root_lump
        lam = jnp.where(flags, lam - 1.0 * gap, jnp.zeros_like(lam))
        slave_proj = jnp.sum(slave_float * lam[:, :, None], axis=1)
        outbound = jnp.dot(block_onehot, weights * slave_proj[pair_slave], precision=high)
        inbound = lax.all_to_all(
            outbound.reshape(peers, mb_dev, qpts), everyone, split_axis=0, concat_axis=0, tiled=True
        )
        if update == ITERS - 1:
            stored, inbound = lax.optimization_barrier((stored, inbound))
        own_load = jnp.sum(inbound, axis=0)
        force = jnp.sum(master_float * own_load[:, None, :], axis=2)
        disp = disp - 0.05 * force
        if update < ITERS - 1:
            own_proj = own_proj - 0.05 * jnp.einsum("mq,mqr->mr", own_load, gram, precision=high)
    return (lam, disp, stored)


def solution(mesh):
    return jax.shard_map(
        on_device,
        mesh=mesh,
        in_specs=(
            P("slave", None, None),
            P(("slave", "master"), None, None),
            P("slave", None),
            P(("slave", "master"), None),
            P("slave", None),
            P("slave", None),
            P(("slave", "master"), None),
            P(("slave", "master")),
            P(("slave", "master")),
            P(("slave", "master")),
            P(("slave", "master")),
            P(("slave", "master"), None),
        ),
        out_specs=(
            P("slave", None),
            P(("slave", "master"), None),
            P(("slave", "master"), None, None),
        ),
        check_vma=False,
    )
```

```python
import functools

import jax
import jax.numpy as jnp
from jax import lax
from jax.experimental import pallas as pl
from jax.experimental.pallas import tpu as pltpu
from jax.sharding import PartitionSpec as P

GAUSS = 16
ITERS = 2
GROUP = 64


def tile_kernel(group, sidx_ref, nidx_ref, mreq_ref, slave_ref, basis_hbm, w_ref, out_ref, recv, sems):
    need = recv.shape[0]

    @pl.when(pl.program_id(0) == 0)
    def _():
        for r in range(need):
            pltpu.make_async_copy(basis_hbm.at[mreq_ref[r]], recv.at[r], sems.at[r]).start()
        for r in range(need):
            pltpu.make_async_copy(basis_hbm.at[0], recv.at[r], sems.at[r]).wait()

    base = pl.program_id(0) * group
    for g in range(group):
        s = sidx_ref[base + g]
        r = nidx_ref[base + g]
        left = slave_ref[s]
        w = w_ref[pl.ds(g, 1), :]
        right = (recv[r].astype(jnp.float32) * w).astype(jnp.bfloat16)
        tile = lax.dot_general(
            left, right, (((1,), (1,)), ((), ())), preferred_element_type=jnp.float32
        )
        out_ref[g] = tile.astype(out_ref.dtype)


def build_tiles(slave_basis, every_basis, request, pair_slave, pair_need, weights):
    pairs = weights.shape[0]
    nodes, qpts = slave_basis.shape[1], slave_basis.shape[2]
    need = request.shape[0]
    group = GROUP
    grid_spec = pltpu.PrefetchScalarGridSpec(
        num_scalar_prefetch=3,
        grid=(pairs // group,),
        in_specs=[
            pl.BlockSpec(slave_basis.shape, lambda i, s, n, m: (0, 0, 0)),
            pl.BlockSpec(memory_space=pl.ANY),
            pl.BlockSpec((group, qpts), lambda i, s, n, m: (i, 0)),
        ],
        out_specs=pl.BlockSpec((group, nodes, nodes), lambda i, s, n, m: (i, 0, 0)),
        scratch_shapes=[
            pltpu.VMEM((need, nodes, qpts), jnp.bfloat16),
            pltpu.SemaphoreType.DMA((need,)),
        ],
    )
    cost = pl.CostEstimate(
        flops=2 * pairs * nodes * nodes * qpts,
        bytes_accessed=pairs * nodes * nodes * 2 + need * nodes * qpts * 2 + pairs * qpts * 4,
        transcendentals=0,
    )
    return pl.pallas_call(
        functools.partial(tile_kernel, group),
        grid_spec=grid_spec,
        out_shape=jax.ShapeDtypeStruct((pairs, nodes, nodes), jnp.bfloat16),
        compiler_params=pltpu.CompilerParams(
            vmem_limit_bytes=48 * 1024 * 1024, dimension_semantics=("arbitrary",)
        ),
        cost_estimate=cost,
    )(pair_slave, pair_need, request, slave_basis, every_basis, weights)


def master_sum(x):
    count = lax.axis_size("master")
    spread = jnp.broadcast_to(x[None], (count,) + x.shape)
    got = lax.all_to_all(spread, "master", split_axis=0, concat_axis=0, tiled=True)
    return jnp.sum(got, axis=0)


def on_device(
    slave_basis,
    master_basis,
    slave_gap,
    master_disp,
    pressure,
    active,
    need_owner,
    need_slot,
    pair_need,
    pair_slave,
    pair_segs,
    pair_weight,
):
    high = lax.Precision.HIGHEST
    everyone = ("slave", "master")
    peers = lax.axis_size(everyone)
    mb_dev = master_basis.shape[0]
    qpts = slave_basis.shape[2]
    owner = need_owner[:, 0]
    request = owner * mb_dev + need_slot
    every_basis = lax.all_gather(master_basis, everyone, axis=0, tiled=True)

    limit = GAUSS * pair_segs
    weights = jnp.where(
        jnp.arange(qpts, dtype=jnp.int32)[None, :] < limit[:, None],
        pair_weight,
        jnp.zeros_like(pair_weight),
    )
    slave_count = slave_basis.shape[0]
    slave_onehot = (
        pair_slave[None, :] == jnp.arange(slave_count, dtype=jnp.int32)[:, None]
    ).astype(jnp.float32)
    mblocks = peers * mb_dev
    pair_block = request[pair_need]
    block_onehot = (
        pair_block[None, :] == jnp.arange(mblocks, dtype=jnp.int32)[:, None]
    ).astype(jnp.float32)
    slave_weight = jnp.dot(slave_onehot, weights, precision=high)
    slave_float = slave_basis.astype(jnp.float32)
    master_float = master_basis.astype(jnp.float32)
    squares = jnp.square(slave_float)
    lump_part = jnp.sum(squares * slave_weight[:, None, :], axis=2)
    gram = jnp.einsum("mnq,mnr->mqr", master_float, master_float, precision=high)

    stored = build_tiles(slave_basis, every_basis, request, pair_slave, pair_need, weights)
    lam = pressure
    disp = master_disp
    flags = active == 1
    root_lump = None
    own_proj = jnp.sum(master_float * disp[:, :, None], axis=1)
    for update in range(ITERS):
        outgoing_proj = jnp.broadcast_to(own_proj[None], (peers,) + own_proj.shape)
        returned = lax.all_to_all(outgoing_proj, everyone, split_axis=0, concat_axis=0, tiled=True)
        pair_terms = weights * returned.reshape(mblocks, qpts)[pair_block]
        slave_terms = jnp.dot(slave_onehot, pair_terms, precision=lax.Precision.HIGH)
        partial_coupled = jnp.sum(slave_float * slave_terms[:, None, :], axis=2)
        if update == 0:
            both = master_sum(jnp.stack([lump_part, partial_coupled]))
            root_lump = jnp.sqrt(1.0 + both[0])
            coupled = both[1]
        else:
            coupled = master_sum(partial_coupled)
        gap = slave_gap - coupled / root_lump
        lam = jnp.where(flags, lam - 1.0 * gap, jnp.zeros_like(lam))
        slave_proj = jnp.sum(slave_float * lam[:, :, None], axis=1)
        outbound = jnp.dot(
            block_onehot, weights * slave_proj[pair_slave], precision=lax.Precision.HIGH
        )
        inbound = lax.all_to_all(
            outbound.reshape(peers, mb_dev, qpts), everyone, split_axis=0, concat_axis=0, tiled=True
        )
        if update == ITERS - 1:
            stored, inbound = lax.optimization_barrier((stored, inbound))
        own_load = jnp.sum(inbound, axis=0)
        force = jnp.sum(master_float * own_load[:, None, :], axis=2)
        disp = disp - 0.05 * force
        if update < ITERS - 1:
            own_proj = own_proj - 0.05 * jnp.einsum("mq,mqr->mr", own_load, gram, precision=high)
    return (lam, disp, stored)


def solution(mesh):
    return jax.shard_map(
        on_device,
        mesh=mesh,
        in_specs=(
            P("slave", None, None),
            P(("slave", "master"), None, None),
            P("slave", None),
            P(("slave", "master"), None),
            P("slave", None),
            P("slave", None),
            P(("slave", "master"), None),
            P(("slave", "master")),
            P(("slave", "master")),
            P(("slave", "master")),
            P(("slave", "master")),
            P(("slave", "master"), None),
        ),
        out_specs=(
            P("slave", None),
            P(("slave", "master"), None),
            P(("slave", "master"), None, None),
        ),
        check_vma=False,
    )
```

```python
import functools

import jax
import jax.numpy as jnp
from jax import lax
from jax.experimental import pallas as pl
from jax.experimental.pallas import tpu as pltpu
from jax.sharding import PartitionSpec as P

GAUSS = 16
ITERS = 2
GROUP = 64


def tile_kernel(group, sidx_ref, nidx_ref, mreq_ref, slave_ref, basis_hbm, w_ref, out_ref, recv, sems):
    need = recv.shape[0]

    @pl.when(pl.program_id(0) == 0)
    def _():
        for r in range(need):
            pltpu.make_async_copy(basis_hbm.at[mreq_ref[r]], recv.at[r], sems.at[r]).start()
        for r in range(need):
            pltpu.make_async_copy(basis_hbm.at[0], recv.at[r], sems.at[r]).wait()

    base = pl.program_id(0) * group
    for g in range(group):
        s = sidx_ref[base + g]
        r = nidx_ref[base + g]
        left = slave_ref[s]
        w = w_ref[pl.ds(g, 1), :]
        right = (recv[r].astype(jnp.float32) * w).astype(jnp.bfloat16)
        tile = lax.dot_general(
            left, right, (((1,), (1,)), ((), ())), preferred_element_type=jnp.float32
        )
        out_ref[g] = tile.astype(out_ref.dtype)


def build_tiles(slave_basis, every_basis, request, pair_slave, pair_need, weights):
    pairs = weights.shape[0]
    nodes, qpts = slave_basis.shape[1], slave_basis.shape[2]
    need = request.shape[0]
    group = GROUP
    grid_spec = pltpu.PrefetchScalarGridSpec(
        num_scalar_prefetch=3,
        grid=(pairs // group,),
        in_specs=[
            pl.BlockSpec(slave_basis.shape, lambda i, s, n, m: (0, 0, 0)),
            pl.BlockSpec(memory_space=pl.ANY),
            pl.BlockSpec((group, qpts), lambda i, s, n, m: (i, 0)),
        ],
        out_specs=pl.BlockSpec((group, nodes, nodes), lambda i, s, n, m: (i, 0, 0)),
        scratch_shapes=[
            pltpu.VMEM((need, nodes, qpts), jnp.bfloat16),
            pltpu.SemaphoreType.DMA((need,)),
        ],
    )
    cost = pl.CostEstimate(
        flops=2 * pairs * nodes * nodes * qpts,
        bytes_accessed=pairs * nodes * nodes * 2 + need * nodes * qpts * 2 + pairs * qpts * 4,
        transcendentals=0,
    )
    return pl.pallas_call(
        functools.partial(tile_kernel, group),
        grid_spec=grid_spec,
        out_shape=jax.ShapeDtypeStruct((pairs, nodes, nodes), jnp.bfloat16),
        compiler_params=pltpu.CompilerParams(
            vmem_limit_bytes=48 * 1024 * 1024, dimension_semantics=("arbitrary",)
        ),
        cost_estimate=cost,
    )(pair_slave, pair_need, request, slave_basis, every_basis, weights)


def couple_kernel(block_ref, proj_ref, w_ref, onehot_ref, basis_ref, out_ref, rows):
    def gather(p, carry):
        rows[pl.ds(p, 1), :] = proj_ref[pl.ds(block_ref[p], 1), :]
        return carry

    lax.fori_loop(0, rows.shape[0], gather, 0)
    terms = rows[...] * w_ref[...]
    summed = jnp.dot(
        onehot_ref[...], terms, precision=lax.Precision.HIGHEST, preferred_element_type=jnp.float32
    )
    out_ref[...] = jnp.sum(basis_ref[...] * summed[:, None, :], axis=2)


def couple(pair_block, proj, weights, onehot, basis):
    grid_spec = pltpu.PrefetchScalarGridSpec(
        num_scalar_prefetch=1,
        grid=(1,),
        in_specs=[
            pl.BlockSpec(proj.shape, lambda i, b: (0, 0)),
            pl.BlockSpec(weights.shape, lambda i, b: (0, 0)),
            pl.BlockSpec(onehot.shape, lambda i, b: (0, 0)),
            pl.BlockSpec(basis.shape, lambda i, b: (0, 0, 0)),
        ],
        out_specs=pl.BlockSpec(basis.shape[:2], lambda i, b: (0, 0)),
        scratch_shapes=[pltpu.VMEM(weights.shape, jnp.float32)],
    )
    return pl.pallas_call(
        couple_kernel,
        grid_spec=grid_spec,
        out_shape=jax.ShapeDtypeStruct(basis.shape[:2], jnp.float32),
        compiler_params=pltpu.CompilerParams(vmem_limit_bytes=32 * 1024 * 1024),
    )(pair_block, proj, weights, onehot, basis)


def master_sum(x):
    count = lax.axis_size("master")
    spread = jnp.broadcast_to(x[None], (count,) + x.shape)
    got = lax.all_to_all(spread, "master", split_axis=0, concat_axis=0, tiled=True)
    return jnp.sum(got, axis=0)


def on_device(
    slave_basis,
    master_basis,
    slave_gap,
    master_disp,
    pressure,
    active,
    need_owner,
    need_slot,
    pair_need,
    pair_slave,
    pair_segs,
    pair_weight,
):
    high = lax.Precision.HIGHEST
    everyone = ("slave", "master")
    peers = lax.axis_size(everyone)
    mb_dev = master_basis.shape[0]
    qpts = slave_basis.shape[2]
    owner = need_owner[:, 0]
    request = owner * mb_dev + need_slot
    every_basis = lax.all_gather(master_basis, everyone, axis=0, tiled=True)

    limit = GAUSS * pair_segs
    weights = jnp.where(
        jnp.arange(qpts, dtype=jnp.int32)[None, :] < limit[:, None],
        pair_weight,
        jnp.zeros_like(pair_weight),
    )
    slave_count = slave_basis.shape[0]
    slave_onehot = (
        pair_slave[None, :] == jnp.arange(slave_count, dtype=jnp.int32)[:, None]
    ).astype(jnp.float32)
    mblocks = peers * mb_dev
    pair_block = request[pair_need]
    block_onehot = (
        pair_block[None, :] == jnp.arange(mblocks, dtype=jnp.int32)[:, None]
    ).astype(jnp.float32)
    slave_weight = jnp.dot(slave_onehot, weights, precision=high)
    slave_float = slave_basis.astype(jnp.float32)
    master_float = master_basis.astype(jnp.float32)
    squares = jnp.square(slave_float)
    lump_part = jnp.sum(squares * slave_weight[:, None, :], axis=2)
    gram = jnp.einsum("mnq,mnr->mqr", master_float, master_float, precision=high)

    stored = build_tiles(slave_basis, every_basis, request, pair_slave, pair_need, weights)
    lam = pressure
    disp = master_disp
    flags = active == 1
    root_lump = None
    own_proj = jnp.sum(master_float * disp[:, :, None], axis=1)
    for update in range(ITERS):
        outgoing_proj = jnp.broadcast_to(own_proj[None], (peers,) + own_proj.shape)
        returned = lax.all_to_all(outgoing_proj, everyone, split_axis=0, concat_axis=0, tiled=True)
        partial_coupled = couple(
            pair_block, returned.reshape(mblocks, qpts), weights, slave_onehot, slave_float
        )
        if update == 0:
            both = master_sum(jnp.stack([lump_part, partial_coupled]))
            root_lump = jnp.sqrt(1.0 + both[0])
            coupled = both[1]
        else:
            coupled = master_sum(partial_coupled)
        gap = slave_gap - coupled / root_lump
        lam = jnp.where(flags, lam - 1.0 * gap, jnp.zeros_like(lam))
        slave_proj = jnp.sum(slave_float * lam[:, :, None], axis=1)
        outbound = jnp.dot(block_onehot, weights * slave_proj[pair_slave], precision=high)
        inbound = lax.all_to_all(
            outbound.reshape(peers, mb_dev, qpts), everyone, split_axis=0, concat_axis=0, tiled=True
        )
        if update == ITERS - 1:
            stored, inbound = lax.optimization_barrier((stored, inbound))
        own_load = jnp.sum(inbound, axis=0)
        force = jnp.sum(master_float * own_load[:, None, :], axis=2)
        disp = disp - 0.05 * force
        if update < ITERS - 1:
            own_proj = own_proj - 0.05 * jnp.einsum("mq,mqr->mr", own_load, gram, precision=high)
    return (lam, disp, stored)


def solution(mesh):
    return jax.shard_map(
        on_device,
        mesh=mesh,
        in_specs=(
            P("slave", None, None),
            P(("slave", "master"), None, None),
            P("slave", None),
            P(("slave", "master"), None),
            P("slave", None),
            P("slave", None),
            P(("slave", "master"), None),
            P(("slave", "master")),
            P(("slave", "master")),
            P(("slave", "master")),
            P(("slave", "master")),
            P(("slave", "master"), None),
        ),
        out_specs=(
            P("slave", None),
            P(("slave", "master"), None),
            P(("slave", "master"), None, None),
        ),
        check_vma=False,
    )
```
